32 devices in a mesh: dp: 8 (over z, core), ctx: 4 (over y, x).
Axes of the slice: x: 2, y: 2, z: 4, core: 2. Of those that a mesh axis runs over, the one named last changes fastest.
Arguments:
- tokens: bfloat16 [4096, 1152], P(('dp', 'ctx')), may hold values from -6 to 6
- lengths: int32 [8, 1], P('dp'), may hold values from 0 to 512, as said below
- w_query: bfloat16 [1152, 1024], P(('dp', 'ctx')), may hold values from -0.1875 to 0.1875
- w_key: bfloat16 [1152, 256], P(('dp', 'ctx')), may hold values from -0.1875 to 0.1875
- w_value: bfloat16 [1152, 256], P(('dp', 'ctx')), may hold values from -0.1875 to 0.1875
- w_out: bfloat16 [1024, 1152], P(('dp', 'ctx')), may hold values from -0.1875 to 0.1875
- w_gate: bfloat16 [1152, 6912], P(('dp', 'ctx')), may hold values from -0.1875 to 0.1875
- w_up: bfloat16 [1152, 6912], P(('dp', 'ctx')), may hold values from -0.1875 to 0.1875
- w_down: bfloat16 [6912, 1152], P(('dp', 'ctx')), may hold values from -0.078125 to 0.078125
- gain_in: bfloat16 [1152], P(('dp', 'ctx')), may hold values from 0.5 to 1.5
- gain_attn_post: bfloat16 [1152], P(('dp', 'ctx')), may hold values from 0.5 to 1.5
- gain_ffn_pre: bfloat16 [1152], P(('dp', 'ctx')), may hold values from 0.5 to 1.5
- gain_ffn_post: bfloat16 [1152], P(('dp', 'ctx')), may hold values from 0.5 to 1.5
- gain_query: bfloat16 [256], P(('dp', 'ctx')), may hold values from 0.5 to 1.5
- gain_key: bfloat16 [256], P(('dp', 'ctx')), may hold values from 0.5 to 1.5
- cotangent: bfloat16 [4096, 1152], P(('dp', 'ctx')), may hold values from -6 to 6
Outputs:
- layer_out: bfloat16 [4096, 1152], P(('dp', 'ctx'))
- input_grad: bfloat16 [4096, 1152], P(('dp', 'ctx'))
- grad_w_query: float32 [1152, 1024], P(('dp', 'ctx'))
- grad_w_key: float32 [1152, 256], P(('dp', 'ctx'))
- grad_w_value: float32 [1152, 256], P(('dp', 'ctx'))
- grad_w_out: float32 [1024, 1152], P(('dp', 'ctx'))
- grad_w_gate: float32 [1152, 6912], P(('dp', 'ctx'))
- grad_w_up: float32 [1152, 6912], P(('dp', 'ctx'))
- grad_w_down: float32 [6912, 1152], P(('dp', 'ctx'))
- grad_gain_in: float32 [1152], P(('dp', 'ctx'))
- grad_gain_attn_post: float32 [1152], P(('dp', 'ctx'))
- grad_gain_ffn_pre: float32 [1152], P(('dp', 'ctx'))
- grad_gain_ffn_post: float32 [1152], P(('dp', 'ctx'))
- grad_gain_query: float32 [256], P(('dp', 'ctx'))
- grad_gain_key: float32 [256], P(('dp', 'ctx'))
The draws below stay inside these ranges and needn't reach their ends.
Inputs may be any that keep to these rules, and one draw needn't show every extreme that they name: Each row lists the lengths of its sequences in order, then zeros; the nonzero ones are 512 or more and sum to 512; some row holds a single sequence.
All inputs are finite; a program needn't handle non-finite values.
Results may differ from the reference program's by a relative error of at most 0.023.
Values may be sent and summed in bfloat16 or wider, within the bound.
No kernel may reach another device: no remote copies, remote signals or barrier semaphores. Data moves between devices by JAX's collectives and lax.ppermute only.
A program may use at most 128 MiB of HBM per device.

```python
import jax
import jax.numpy as jnp
from jax import lax

D = 1152
FF = 6912
HEADS = 4
HD = 256
TOK_DEV = 128
MIN_LEN = 512
QW = 1024
ROW_LEN = 512
TOKENS = 4096
UNIT_GROUP = 216
N_DP = 8
N_CTX = 4


def draw_lengths(key, part):
    row_count = N_DP
    slot_count = ROW_LEN // MIN_LEN
    first_key, second_key, third_key = jax.random.split(key, 3)
    counts = jax.random.randint(first_key, (row_count,), 1, slot_count + 1)
    single_row = jax.random.randint(second_key, (), 0, row_count)
    counts = jnp.where(jnp.arange(row_count) == single_row, 1, counts)
    extra = ROW_LEN - counts * MIN_LEN
    cut_points = jax.random.randint(third_key, (row_count, slot_count - 1), 0, 1 << 30) % (extra[:, None] + 1)
    cut_index = jnp.arange(slot_count - 1)[None, :]
    cut_points = jnp.where(cut_index < counts[:, None] - 1, cut_points, extra[:, None])
    cut_points = jnp.sort(cut_points, axis=1)
    edges = jnp.concatenate([jnp.zeros((row_count, 1), jnp.int32), cut_points.astype(jnp.int32), extra[:, None].astype(jnp.int32)], axis=1)
    spans = edges[:, 1:] - edges[:, :-1]
    used = jnp.arange(slot_count)[None, :] < counts[:, None]
    return jnp.where(used, MIN_LEN + spans, 0).astype(jnp.int32)


def levels(own_key, shape, pieces, least, largest):
    def one(dim, shards_of):
        heights = jax.random.uniform(jax.random.fold_in(jax.random.fold_in(own_key, 6), dim), (shards_of,), jnp.float32, least / len(pieces), largest / len(pieces))
        return jnp.repeat(jnp.exp(heights), shape[dim] // shards_of).reshape((-1,) + (1,) * (len(shape) - dim - 1))

    factor_of = one(*pieces[0])
    for cut in pieces[1:]:
        factor_of = factor_of * one(*cut)
    return factor_of


def noise(key, extent, scale, most, pieces=(), kind=jnp.bfloat16):
    level = levels(key, extent, pieces, -0.22, 0.18) if pieces else 1.0
    values = jax.random.normal(key, extent, jnp.float32) * scale * level
    return jnp.minimum(jnp.maximum(values, -most), most).astype(kind)


def setup_inputs(seed: int = 0) -> dict:
    key_of = jax.random.split(jax.random.key(seed), 17)
    tokens = noise(key_of[0], (TOKENS, D), 1.0, 6.0, ((0, 32),))
    lengths = draw_lengths(jax.random.fold_in(key_of[16], 71), 0)
    w_query = noise(key_of[2], (D, QW), D ** -0.5, 0.1875, ((0, 32),))
    w_key = noise(key_of[3], (D, HD), D ** -0.5, 0.1875, ((0, 32),))
    w_value = noise(key_of[4], (D, HD), D ** -0.5, 0.1875, ((0, 32),))
    w_out = noise(key_of[5], (QW, D), QW ** -0.5, 0.1875, ((0, 32),))
    w_gate = noise(key_of[6], (D, FF), D ** -0.5, 0.1875, ((0, 32),))
    w_up = noise(key_of[7], (D, FF), D ** -0.5, 0.1875, ((0, 32),))
    w_down = noise(key_of[8], (FF, D), FF ** -0.5, 0.078125, ((0, 32),))
    gain_in = jnp.clip(1.0 + 0.1 * jax.random.normal(key_of[9], (D,), jnp.float32), 0.5, 1.5).astype(jnp.bfloat16)
    gain_attn_post = jnp.clip(1.0 + 0.1 * jax.random.normal(key_of[10], (D,), jnp.float32), 0.5, 1.5).astype(jnp.bfloat16)
    gain_ffn_pre = jnp.clip(1.0 + 0.1 * jax.random.normal(key_of[11], (D,), jnp.float32), 0.5, 1.5).astype(jnp.bfloat16)
    gain_ffn_post = jnp.clip(1.0 + 0.1 * jax.random.normal(key_of[12], (D,), jnp.float32), 0.5, 1.5).astype(jnp.bfloat16)
    gain_query = jnp.clip(1.0 + 0.1 * jax.random.normal(key_of[13], (HD,), jnp.float32), 0.5, 1.5).astype(jnp.bfloat16)
    gain_key = jnp.clip(1.0 + 0.1 * jax.random.normal(key_of[14], (HD,), jnp.float32), 0.5, 1.5).astype(jnp.bfloat16)
    cotangent = noise(key_of[15], (TOKENS, D), 1.0, 6.0, ((0, 32),))
    return dict(tokens=tokens, lengths=lengths, w_query=w_query, w_key=w_key, w_value=w_value, w_out=w_out, w_gate=w_gate, w_up=w_up, w_down=w_down, gain_in=gain_in, gain_attn_post=gain_attn_post, gain_ffn_pre=gain_ffn_pre, gain_ffn_post=gain_ffn_post, gain_query=gain_query, gain_key=gain_key, cotangent=cotangent)


NORM_EPS = 1e-06
ROPE_BASE = 1000000.0
MASKED_SCORE = -1e+30

@jax.custom_vjp
def low(v):
    return lax.optimization_barrier(v.astype(jnp.bfloat16)).astype(jnp.float32)

@jax.custom_vjp
def low_back(v):
    return v

def low_keep(v):
    return (low(v), None)

def low_pass(kept, grad):
    return (grad,)

def back_keep(v):
    return (v, None)

def back_low(kept, grad):
    return (low(grad),)
low.defvjp(low_keep, low_pass)
low_back.defvjp(back_keep, back_low)

def matmul_high(left, right):
    return jnp.dot(left, right, precision=lax.Precision.HIGHEST, preferred_element_type=jnp.float32)

def rms_norm(values_in, gain):
    return values_in * lax.rsqrt(lax.optimization_barrier(jnp.mean(values_in * values_in, axis=-1, keepdims=True)) + NORM_EPS) * gain

def layout_places(slots, tok_dev, n_ctx):
    half_len = tok_dev // 2
    slot_owner = slots // tok_dev
    slot_inner = slots % tok_dev
    block_id = jnp.where(slot_inner < half_len, slot_owner, 2 * n_ctx - 1 - slot_owner)
    return (block_id * half_len + slot_inner % half_len).astype(jnp.int32)

def segment_info(places, seq_lengths):
    ends = jnp.cumsum(seq_lengths).astype(jnp.int32)
    passed = places[:, None] >= ends[None, :]
    segment = lax.optimization_barrier(jnp.sum(passed.astype(jnp.int32), axis=-1)).astype(jnp.int32)
    start = lax.optimization_barrier(jnp.sum(jnp.where(passed, seq_lengths[None, :], 0), axis=-1)).astype(jnp.int32)
    return (segment, (places - start).astype(jnp.int32))

def rope_tables(relative):
    head_half = HD // 2
    freqs = ROPE_BASE ** (-(jnp.arange(head_half, dtype=jnp.float32) * 2.0 / HD))
    angles = relative.astype(jnp.float32)[:, None] * freqs[None, :]
    cosine = jnp.concatenate([jnp.cos(angles), jnp.cos(angles)], axis=-1)
    sine = jnp.concatenate([jnp.sin(angles), jnp.sin(angles)], axis=-1)
    return (cosine, sine)

def rotate(values_in, cosine, sine):
    head_half = values_in.shape[-1] // 2
    turned = jnp.concatenate([-values_in[..., head_half:], values_in[..., :head_half]], axis=-1)
    return values_in * cosine + turned * sine

def ffn_piece(gate, upward):
    return jax.nn.gelu(gate, approximate=True) * upward

def group_columns(weight, group):
    return weight.reshape(D, N_DP, N_CTX, UNIT_GROUP)[:, :, group, :].reshape(D, N_DP * UNIT_GROUP)

def group_rows(weight, group):
    return weight.reshape(N_DP, N_CTX, UNIT_GROUP, D)[:, group].reshape(N_DP * UNIT_GROUP, D)

def row_layer(row_in, seq_lengths, params):
    w_query, w_key, w_value, w_out, w_gate, w_up, w_down, gain_in, gain_attn_post, gain_ffn_pre, gain_ffn_post, gain_query, gain_key = params
    places = layout_places(jnp.arange(ROW_LEN, dtype=jnp.int32), TOK_DEV, N_CTX)
    segment, relative = segment_info(places, seq_lengths)
    cosine, sine = rope_tables(relative)
    normed = low(rms_norm(row_in, gain_in))
    query_lin = low_back(matmul_high(normed, w_query)).reshape(ROW_LEN, HEADS, HD)
    key_lin = low_back(matmul_high(normed, w_key))
    value_rows = low(low_back(matmul_high(normed, w_value)))
    query_rows = low(rotate(rms_norm(query_lin, gain_query), cosine[:, None, :], sine[:, None, :]))
    key_rows = low(rotate(rms_norm(key_lin, gain_key), cosine, sine))
    raw = jnp.einsum('qhd,kd->hqk', query_rows, key_rows, precision=lax.Precision.HIGHEST) * HD ** (-0.5)
    raw = low_back(raw)
    allowed = (segment[:, None] == segment[None, :]) & (places[None, :] <= places[:, None])
    scores = jnp.where(allowed[None], raw, MASKED_SCORE)
    probs = jax.nn.softmax(scores, axis=-1)
    attended = jnp.einsum('hqk,kd->qhd', low(probs), value_rows, precision=lax.Precision.HIGHEST)
    attended = low_back(low(attended.reshape(ROW_LEN, HEADS * HD)))
    branch_attn = low_back(matmul_high(attended, w_out))
    hidden_one = row_in + rms_norm(branch_attn, gain_attn_post)
    ffn_in = low(rms_norm(hidden_one, gain_ffn_pre))
    total = jnp.zeros((ROW_LEN, D), jnp.float32)
    for group in range(N_CTX):
        group_in = low_back(ffn_in)
        gate = low_back(matmul_high(group_in, group_columns(w_gate, group)))
        upward = low_back(matmul_high(group_in, group_columns(w_up, group)))
        hidden = low(ffn_piece(gate, upward))
        total = total + low(matmul_high(hidden, group_rows(w_down, group)))
    branch_ffn = low_back(total)
    return hidden_one + rms_norm(branch_ffn, gain_ffn_post)

def reference(tokens, lengths, w_query, w_key, w_value, w_out, w_gate, w_up, w_down, gain_in, gain_attn_post, gain_ffn_pre, gain_ffn_post, gain_query, gain_key, cotangent):
    params = tuple((entry.astype(jnp.float32) for entry in (w_query, w_key, w_value, w_out, w_gate, w_up, w_down, gain_in, gain_attn_post, gain_ffn_pre, gain_ffn_post, gain_query, gain_key)))
    rows_in = tokens.astype(jnp.float32).reshape(N_DP, ROW_LEN, D)
    cot_rows = cotangent.astype(jnp.float32).reshape(N_DP, ROW_LEN, D)

    def forward(rows, weights):

        def one_row(pair):
            return jax.checkpoint(row_layer)(pair[0], pair[1], weights)
        return lax.map(one_row, (rows, lengths))
    out_rows, pull = jax.vjp(forward, rows_in, params)
    grad_rows, grads = pull(cot_rows)
    return (out_rows.reshape(TOKENS, D).astype(jnp.bfloat16), grad_rows.reshape(TOKENS, D).astype(jnp.bfloat16), grads[0], grads[1], grads[2], grads[3], grads[4], grads[5], grads[6], grads[7], grads[8], grads[9], grads[10], grads[11], grads[12])
```

```python
import jax
import jax.numpy as jnp
from jax import lax
from jax.sharding import PartitionSpec as P

HEADS = 4
HD = 256
QW = HEADS * HD


NORM_EPS = 1e-06
ROPE_BASE = 1000000.0
MASKED_SCORE = -1e30
F32 = jnp.float32
BF16 = jnp.bfloat16


def rms_norm(values_in, gain):
    return (
        values_in
        * lax.rsqrt(jnp.mean(values_in * values_in, axis=-1, keepdims=True) + NORM_EPS)
        * gain
    )


def places_of(owner, inner, tok_dev, n_ctx):
    half_len = tok_dev // 2
    block_id = jnp.where(inner < half_len, owner, 2 * n_ctx - 1 - owner)
    return block_id * half_len + inner % half_len


def segment_info(places, seq_lengths):
    ends = jnp.cumsum(seq_lengths)
    passed = places[:, None] >= ends[None, :]
    segment = jnp.sum(passed.astype(jnp.int32), axis=-1)
    start = jnp.sum(jnp.where(passed, seq_lengths[None, :], 0), axis=-1)
    return (segment, places - start)


def rope_tables(relative):
    head_half = HD // 2
    freqs = ROPE_BASE ** (-(jnp.arange(head_half, dtype=F32) * 2.0 / HD))
    angles = relative.astype(F32)[:, None] * freqs[None, :]
    cosine = jnp.concatenate([jnp.cos(angles), jnp.cos(angles)], axis=-1)
    sine = jnp.concatenate([jnp.sin(angles), jnp.sin(angles)], axis=-1)
    return (cosine, sine)


def rotate(values_in, cosine, sine):
    head_half = values_in.shape[-1] // 2
    turned = jnp.concatenate([-values_in[..., head_half:], values_in[..., :head_half]], axis=-1)
    return values_in * cosine + turned * sine


def ffn_piece(gate, upward):
    return jax.nn.gelu(gate, approximate=True) * upward


def matmul_fast(left, right):
    return jnp.dot(left, right, preferred_element_type=F32)


def left_transposed(left, right):
    return jnp.einsum("ta,tb->ab", left, right, preferred_element_type=F32)


def right_transposed(left, right):
    return jnp.einsum("ta,ba->tb", left, right, preferred_element_type=F32)


def pad_rows(values_in, rows):
    return jnp.pad(values_in, ((0, rows - values_in.shape[0]), (0, 0)))


def body(
    tokens,
    lengths,
    w_query,
    w_key,
    w_value,
    w_out,
    w_gate,
    w_up,
    w_down,
    gain_in,
    gain_attn_post,
    gain_ffn_pre,
    gain_ffn_post,
    gain_query,
    gain_key,
    cotangent,
):
    n_ctx = lax.axis_size("ctx")
    n_dp = lax.axis_size("dp")
    n_z = n_dp // 2
    n_dev = n_dp * n_ctx
    tok_dev, width = tokens.shape
    dp = lax.axis_index("dp")
    ctx = lax.axis_index("ctx")
    zi = dp // 2
    core = dp % 2
    scale = HD ** (-0.5)

    def swap_z(values_in, j):
        return lax.ppermute(values_in, "dp", [(d, d ^ (2 * j)) for d in range(n_dp)])

    def swap_core(values_in):
        return lax.ppermute(values_in, "dp", [(d, d ^ 1) for d in range(n_dp)])

    def swap_c(values_in, j):
        return lax.ppermute(values_in, "ctx", [(i, i ^ j) for i in range(n_ctx)])

    def gather_z(values_in):
        return jnp.concatenate([values_in] + [swap_z(values_in, j) for j in range(1, n_z)], axis=0)

    def gather_c(values_in):
        return jnp.concatenate([values_in] + [swap_c(values_in, j) for j in range(1, n_ctx)], axis=0)

    def gather_core(values_in):
        return jnp.concatenate([values_in, swap_core(values_in)], axis=0)

    def scatter_core(values_in):
        half = values_in.shape[0] // 2
        return values_in[:half] + swap_core(values_in[half:].astype(BF16)).astype(F32)

    def scatter_by(values_in, n, swap):
        rows = values_in.shape[0] // n
        total = values_in[:rows]
        for j in range(1, n):
            total = total + swap(values_in[j * rows : (j + 1) * rows].astype(BF16), j).astype(F32)
        return total

    def scatter_c(values_in):
        return scatter_by(values_in, n_ctx, swap_c)

    def scatter_z(values_in):
        return scatter_by(values_in, n_z, swap_z)

    slots = jnp.arange(n_dev, dtype=jnp.int32)
    slot_dp = dp ^ (slots // (n_dev // 2) + 2 * (slots % n_z))
    slot_ctx = ctx ^ ((slots // n_z) % n_ctx)
    slot_dev = slot_dp * n_ctx + slot_ctx

    def one_hot(total, rows, padded):
        inner = jnp.arange(padded, dtype=jnp.int32)
        natural = jnp.where(inner[None, :] < rows, slot_dev[:, None] * rows + inner[None, :], -1)
        picks = jnp.arange(total, dtype=jnp.int32)[:, None] == natural.reshape(1, -1)
        return picks.astype(BF16)

    rows_w = w_query.shape[0]
    rows_p = -(-rows_w // 8) * 8
    rows_o = w_out.shape[0]
    rows_q = gain_query.shape[0]
    hot_w = one_hot(width, rows_w, rows_p)
    hot_o = one_hot(QW, rows_o, rows_o)
    hot_q = one_hot(HD, rows_q, rows_p)

    def column(gain):
        return jnp.pad(gain, (0, rows_w - gain.shape[0]))[:, None]

    gain_cols = jnp.concatenate(
        [
            column(g)
            for g in (gain_in, gain_attn_post, gain_ffn_pre, gain_ffn_post, gain_query, gain_key)
        ],
        axis=1,
    )
    w_rows = jnp.concatenate([w_query, w_key, w_value], axis=1)
    n_qkv = w_rows.shape[1]
    payload = jnp.concatenate([w_rows, jnp.pad(gain_cols, ((0, 0), (0, 128 - 6)))], axis=1)
    full_w = gather_core(gather_c(gather_z(pad_rows(payload, rows_p))))
    full_qkv = full_w[:, :n_qkv]
    full_gains = full_w[:, n_qkv:]
    gains_d = jnp.einsum("kg,dk->gd", full_gains, hot_w, preferred_element_type=F32)
    gains_h = jnp.einsum("kg,dk->gd", full_gains, hot_q, preferred_element_type=F32)
    norm_in, norm_attn_post, norm_ffn_pre, norm_ffn_post = (gains_d[i] for i in range(4))
    norm_query, norm_key = gains_h[4], gains_h[5]
    full_out = gather_core(gather_c(gather_z(w_out)))

    cols = w_gate.shape[1] // n_z

    def group_weight(weight):
        stack = jnp.stack([pad_rows(weight[:, g * cols : (g + 1) * cols], rows_p) for g in range(n_z)])
        pieces = [lax.dynamic_index_in_dim(stack, zi ^ j, keepdims=False) for j in range(n_z)]
        joined = jnp.concatenate(
            [pieces[0]] + [swap_z(pieces[j], j) for j in range(1, n_z)], axis=0
        )
        return gather_core(gather_c(joined))

    full_gate = group_weight(w_gate)
    full_up = group_weight(w_up)
    units = w_down.shape[0]
    down_plane = jnp.zeros((n_ctx, units, width), BF16)
    down_plane = lax.dynamic_update_index_in_dim(down_plane, w_down, ctx, 0)
    for j in range(1, n_ctx):
        down_plane = lax.dynamic_update_index_in_dim(down_plane, swap_c(w_down, j), ctx ^ j, 0)
    full_down = jnp.zeros((2, n_ctx, units, width), BF16)
    full_down = lax.dynamic_update_index_in_dim(full_down, down_plane, core, 0)
    full_down = lax.dynamic_update_index_in_dim(full_down, swap_core(down_plane), 1 - core, 0)
    full_down = full_down.reshape(2 * n_ctx * units, width)

    seq_lengths = lengths[0]
    inner = jnp.arange(tok_dev, dtype=jnp.int32)
    local_places = places_of(jnp.full_like(inner, ctx), inner, tok_dev, n_ctx)
    row_owner = ctx ^ jnp.arange(n_ctx, dtype=jnp.int32)
    row_places = places_of(row_owner[:, None], inner[None, :], tok_dev, n_ctx).reshape(-1)
    local_segment, local_relative = segment_info(local_places, seq_lengths)
    row_segment, row_relative = segment_info(row_places, seq_lengths)
    cosine, sine = rope_tables(local_relative)

    def query_piece(query_lin, gain):
        shaped = query_lin.reshape(tok_dev, HEADS, HD)
        return rotate(rms_norm(shaped, gain), cosine[:, None, :], sine[:, None, :])

    def key_piece(key_lin, gain):
        return rotate(rms_norm(key_lin, gain), cosine, sine)

    layer_in = tokens.astype(F32)
    normed, pull_in = jax.vjp(lambda v: rms_norm(v, norm_in), layer_in)
    normed_slots = matmul_fast(normed.astype(BF16), hot_w).astype(BF16)
    qkv_lin = matmul_fast(normed_slots, full_qkv)
    query_lin = qkv_lin[:, :QW]
    key_lin = qkv_lin[:, QW : QW + HD]
    value_lin = qkv_lin[:, QW + HD :]
    query_rot, pull_query = jax.vjp(query_piece, query_lin, norm_query)
    key_rot, pull_key = jax.vjp(key_piece, key_lin, norm_key)
    query_low = query_rot.astype(BF16).reshape(tok_dev * HEADS, HD)
    row_kv = gather_c(jnp.concatenate([key_rot.astype(BF16), value_lin.astype(BF16)], axis=1))
    row_keys = row_kv[:, :HD]
    row_values = row_kv[:, HD:]
    query_segment = jnp.repeat(local_segment, HEADS)
    query_places = jnp.repeat(local_places, HEADS)
    allowed = (query_segment[:, None] == row_segment[None, :]) & (
        row_places[None, :] <= query_places[:, None]
    )

    def masked_scores():
        raw = right_transposed(query_low, row_keys) * scale
        return jnp.where(allowed, raw, MASKED_SCORE)

    scores = masked_scores()
    row_max = jnp.max(scores, axis=-1, keepdims=True)
    expo = jnp.exp(scores - row_max)
    total = jnp.sum(expo, axis=-1, keepdims=True)
    probs = expo / total
    probs_low = probs.astype(BF16)
    attended = matmul_fast(probs_low, row_values)
    attended_low = attended.astype(BF16).reshape(tok_dev, QW)
    attended_slots = matmul_fast(attended_low, hot_o).astype(BF16)
    branch_attn = matmul_fast(attended_slots, full_out)
    post_attn, pull_attn_post = jax.vjp(rms_norm, branch_attn, norm_attn_post)
    hidden_one = layer_in + post_attn
    ffn_in, pull_ffn_pre = jax.vjp(rms_norm, hidden_one, norm_ffn_pre)

    ffn_rows = gather_z(ffn_in.astype(BF16))
    ffn_source = matmul_fast(ffn_rows, hot_w).astype(BF16)
    gate = matmul_fast(ffn_source, full_gate)
    upward = matmul_fast(ffn_source, full_up)
    hidden, pull_ffn = jax.vjp(ffn_piece, gate, upward)
    hidden_low = hidden.astype(BF16)
    branch_ffn = scatter_z(matmul_fast(hidden_low, full_down))
    post_ffn, pull_ffn_post = jax.vjp(rms_norm, branch_ffn, norm_ffn_post)
    layer_out = (hidden_one + post_ffn).astype(BF16)

    grad_out = cotangent.astype(F32)
    grad_branch_ffn, grad_ffn_post = pull_ffn_post(grad_out)
    grad_branch_rows = gather_z(grad_branch_ffn.astype(BF16))
    grad_hidden = right_transposed(grad_branch_rows, full_down)
    grad_gate, grad_upward = pull_ffn(grad_hidden)
    grad_gate_low = grad_gate.astype(BF16)
    grad_upward_low = grad_upward.astype(BF16)
    grad_ffn_terms = right_transposed(grad_gate_low, full_gate) + right_transposed(
        grad_upward_low, full_up
    )
    grad_ffn_natural = right_transposed(grad_ffn_terms.astype(BF16), hot_w)
    grad_ffn_in = scatter_z(grad_ffn_natural)
    grad_down = left_transposed(hidden_low, grad_branch_rows)
    grad_gate_w = left_transposed(ffn_source, grad_gate_low)
    grad_up_w = left_transposed(ffn_source, grad_upward_low)

    def scatter_group(grad_w):
        mine = scatter_c(scatter_core(grad_w))
        placed = jnp.zeros((n_z, rows_p, cols), F32)
        placed = lax.dynamic_update_index_in_dim(placed, mine[:rows_p], zi, 0)
        for j in range(1, n_z):
            got = swap_z(mine[j * rows_p : (j + 1) * rows_p].astype(BF16), j).astype(F32)
            placed = lax.dynamic_update_index_in_dim(placed, got, zi ^ j, 0)
        return jnp.concatenate([placed[g, :rows_w] for g in range(n_z)], axis=1)

    down_blocks = grad_down.reshape(2, n_ctx, units, width)
    down_half = lax.dynamic_index_in_dim(down_blocks, core, keepdims=False) + swap_core(
        lax.dynamic_index_in_dim(down_blocks, 1 - core, keepdims=False).astype(BF16)
    ).astype(F32)
    out_down = lax.dynamic_index_in_dim(down_half, ctx, keepdims=False)
    for j in range(1, n_ctx):
        sent = lax.dynamic_index_in_dim(down_half, ctx ^ j, keepdims=False).astype(BF16)
        out_down = out_down + swap_c(sent, j).astype(F32)
    out_gate = scatter_group(grad_gate_w)
    out_up = scatter_group(grad_up_w)

    grad_hidden_part, grad_ffn_pre = pull_ffn_pre(grad_ffn_in)
    grad_hidden_one = grad_out + grad_hidden_part
    grad_branch_attn, grad_attn_post = pull_attn_post(grad_hidden_one)
    grad_attn_low = grad_branch_attn.astype(BF16)
    grad_out_w = left_transposed(attended_slots, grad_attn_low)
    out_w_out = scatter_z(scatter_c(scatter_core(grad_out_w)))
    grad_attended_slots = right_transposed(grad_attn_low, full_out).astype(BF16)
    grad_attended_low = right_transposed(grad_attended_slots, hot_o).astype(BF16)
    grad_attended_low = grad_attended_low.reshape(tok_dev * HEADS, HD)
    grad_probs = right_transposed(grad_attended_low, row_values)
    delta = jnp.sum(grad_probs * probs, axis=-1, keepdims=True)
    grad_scores_low = (probs * (grad_probs - delta)).astype(BF16)
    key_part = left_transposed(grad_scores_low, query_low) * scale
    value_part = left_transposed(probs_low, grad_attended_low)
    grad_kv = scatter_c(jnp.concatenate([key_part, value_part], axis=1))
    grad_query_rows = matmul_fast(grad_scores_low, row_keys) * scale
    grad_query_lin, grad_norm_query = pull_query(grad_query_rows.reshape(tok_dev, HEADS, HD))
    grad_key_lin, grad_norm_key = pull_key(grad_kv[:, :HD])
    grad_qkv_low = jnp.concatenate(
        [grad_query_lin, grad_key_lin, grad_kv[:, HD:]], axis=1
    ).astype(BF16)
    grad_qkv_w = left_transposed(normed_slots, grad_qkv_low)
    grads_d = jnp.stack([grad_attn_post, grad_ffn_pre, grad_ffn_post]).astype(BF16)
    grads_h = jnp.stack([grad_norm_query, grad_norm_key]).astype(BF16)
    grad_cols = jnp.concatenate(
        [
            jnp.einsum("dk,gd->kg", hot_w, grads_d, preferred_element_type=F32),
            jnp.einsum("dk,gd->kg", hot_q, grads_h, preferred_element_type=F32),
        ],
        axis=1,
    )
    grad_payload = jnp.concatenate([grad_qkv_w, jnp.pad(grad_cols, ((0, 0), (0, 128 - 5)))], axis=1)
    mine_w = scatter_z(scatter_c(scatter_core(grad_payload)))[:rows_w]
    grad_normed = right_transposed(
        right_transposed(grad_qkv_low, full_qkv).astype(BF16), hot_w
    )
    (grad_in_part,) = pull_in(grad_normed)
    input_grad = (grad_hidden_one + grad_in_part).astype(BF16)
    out_gain_in = jnp.sum(w_rows.astype(F32) * mine_w[:, :n_qkv], axis=1) / gain_in.astype(F32)
    gain_out = mine_w[:, n_qkv:]
    return (
        layer_out,
        input_grad,
        mine_w[:, :QW],
        mine_w[:, QW : QW + HD],
        mine_w[:, QW + HD : n_qkv],
        out_w_out,
        out_gate,
        out_up,
        out_down,
        out_gain_in,
        gain_out[:, 0],
        gain_out[:, 1],
        gain_out[:, 2],
        gain_out[:rows_q, 3],
        gain_out[:rows_q, 4],
    )


def solution(mesh):
    split = P(("dp", "ctx"), None)
    split_1d = P(("dp", "ctx"))
    in_specs = (split, P("dp", None)) + (split,) * 7 + (split_1d,) * 6 + (split,)
    out_specs = (split,) * 9 + (split_1d,) * 6
    return jax.shard_map(body, mesh=mesh, in_specs=in_specs, out_specs=out_specs, check_vma=False)
```

```python
import jax
import jax.numpy as jnp
from jax import lax
from jax.experimental import pallas as pl
from jax.experimental.layout import Layout, with_layout_constraint
from jax.experimental.pallas import tpu as pltpu
from jax.sharding import PartitionSpec as P

HEADS = 4
HD = 256
QW = HEADS * HD


NORM_EPS = 1e-06
ROPE_BASE = 1000000.0
MASKED_SCORE = -1e30
F32 = jnp.float32
BF16 = jnp.bfloat16


def rms_norm(values_in, gain):
    return (
        values_in
        * lax.rsqrt(jnp.mean(values_in * values_in, axis=-1, keepdims=True) + NORM_EPS)
        * gain
    )


def places_of(owner, inner, tok_dev, n_ctx):
    half_len = tok_dev // 2
    block_id = jnp.where(inner < half_len, owner, 2 * n_ctx - 1 - owner)
    return block_id * half_len + inner % half_len


def segment_info(places, seq_lengths):
    ends = jnp.cumsum(seq_lengths)
    passed = places[:, None] >= ends[None, :]
    segment = jnp.sum(passed.astype(jnp.int32), axis=-1)
    start = jnp.sum(jnp.where(passed, seq_lengths[None, :], 0), axis=-1)
    return (segment, places - start)


def rope_tables(relative):
    head_half = HD // 2
    freqs = ROPE_BASE ** (-(jnp.arange(head_half, dtype=F32) * 2.0 / HD))
    angles = relative.astype(F32)[:, None] * freqs[None, :]
    cosine = jnp.concatenate([jnp.cos(angles), jnp.cos(angles)], axis=-1)
    sine = jnp.concatenate([jnp.sin(angles), jnp.sin(angles)], axis=-1)
    return (cosine, sine)


def rotate(values_in, cosine, sine):
    head_half = values_in.shape[-1] // 2
    turned = jnp.concatenate([-values_in[..., head_half:], values_in[..., :head_half]], axis=-1)
    return values_in * cosine + turned * sine


def ffn_piece(gate, upward):
    return jax.nn.gelu(gate, approximate=True) * upward


def matmul_fast(left, right):
    return jnp.dot(left, right, preferred_element_type=F32)


def left_transposed(left, right):
    return jnp.einsum("ta,tb->ab", left, right, preferred_element_type=F32)


def right_transposed(left, right):
    return jnp.einsum("ta,ba->tb", left, right, preferred_element_type=F32)


def device_columns(k, c, t, n_y, units):
    start = (((t // n_y) * 4 + (k // 2) * 2 + c) * 2 * n_y + (t % n_y) * 2 + k % 2) * units
    return slice(start, start + units)


def split_columns(w_gate, w_up, core, n_t, n_y, units):
    rows = w_gate.shape[0]

    def kernel(core_ref, gate_ref, up_ref, out_ref):
        own = core_ref[0]
        for i, ref in enumerate((gate_ref, up_ref)):
            for c in range(2):
                for k in range(4):
                    for t in range(n_t):
                        out_ref[own ^ c, k, i, :, t * units : (t + 1) * units] = ref[
                            :, device_columns(k, c, t, n_y, units)
                        ]

    vmem = pl.BlockSpec(memory_space=pltpu.VMEM)
    return pl.pallas_call(
        kernel,
        out_shape=jax.ShapeDtypeStruct((2, 4, 2, rows, n_t * units), BF16),
        in_specs=[pl.BlockSpec(memory_space=pltpu.SMEM), vmem, vmem],
        out_specs=vmem,
        name="split_columns",
    )(jnp.reshape(core, (1,)), w_gate, w_up)


def join_columns(mine, other, zx, core, n_t, n_y, units):
    rows = mine.shape[2]

    def kernel(place_ref, mine_ref, other_ref, *outs):
        for i, out_ref in enumerate(outs):
            for k in range(4):
                own_core = mine_ref[place_ref[0] ^ k, i].astype(F32)
                other_core = other_ref[place_ref[0] ^ k, i].astype(F32)
                for c in range(2):
                    found = jnp.where(place_ref[1] == c, own_core, other_core)
                    for t in range(n_t):
                        out_ref[:, device_columns(k, c, t, n_y, units)] = found[
                            :, t * units : (t + 1) * units
                        ]

    vmem = pl.BlockSpec(memory_space=pltpu.VMEM)
    out = jax.ShapeDtypeStruct((rows, 8 * n_t * units), F32)
    return pl.pallas_call(
        kernel,
        out_shape=(out, out),
        in_specs=[pl.BlockSpec(memory_space=pltpu.SMEM), vmem, vmem],
        out_specs=(vmem, vmem),
        name="join_columns",
    )(jnp.stack([zx, core]), mine, other)


def body(
    tokens,
    lengths,
    w_query,
    w_key,
    w_value,
    w_out,
    w_gate,
    w_up,
    w_down,
    gain_in,
    gain_attn_post,
    gain_ffn_pre,
    gain_ffn_post,
    gain_query,
    gain_key,
    cotangent,
):
    n_ctx = lax.axis_size("ctx")
    n_dp = lax.axis_size("dp")
    n_y = n_ctx // 2
    n_zh = n_dp // 4
    n_t = n_y * n_zh
    n_dev = n_dp * n_ctx
    tok_dev, width = tokens.shape
    dp = lax.axis_index("dp")
    ctx = lax.axis_index("ctx")
    zh, zl, core = dp // 4, (dp // 2) % 2, dp % 2
    y, x = ctx // 2, ctx % 2
    zx = zl * 2 + x
    scale = HD ** (-0.5)

    def move(values_in, dzh=0, dzl=0, dcore=0, dy=0, dx=0):
        pairs = [
            (d * n_ctx + c, (d ^ (4 * dzh + 2 * dzl + dcore)) * n_ctx + (c ^ (2 * dy + dx)))
            for d in range(n_dp)
            for c in range(n_ctx)
        ]
        return lax.ppermute(values_in, ("dp", "ctx"), pairs)

    def near(values_in, k):
        return move(values_in, dzl=k // 2, dx=k % 2)

    def pick(values_in, index, axis=0):
        return lax.dynamic_index_in_dim(values_in, index, axis, keepdims=False)

    def put(buffer, values_in, index, axis=0):
        return lax.dynamic_update_index_in_dim(buffer, values_in, index, axis)

    def after(values_in, *others):
        return lax.optimization_barrier((values_in,) + others)[0]

    def gather_zh(rows):
        return after(
            jnp.concatenate([rows] + [move(rows, dzh=j) for j in range(1, n_zh)], axis=0)
        )

    def gather_y(rows):
        return after(jnp.concatenate([rows] + [move(rows, dy=j) for j in range(1, n_y)], axis=0))

    def gather_near(rows):
        return [rows] + [near(rows, k) for k in range(1, 4)]

    def join_cores(own):
        return jnp.concatenate(own + [move(p, dcore=1) for p in own], axis=0)

    def low_sum(total, got):
        return total + got.astype(F32)

    def scatter_blocks(values_in, n, send):
        rows = values_in.shape[0] // n
        total = values_in[:rows]
        for j in range(1, n):
            total = low_sum(total, send(values_in[j * rows : (j + 1) * rows].astype(BF16), j))
        return total

    def scatter_y(values_in):
        return scatter_blocks(values_in, n_y, lambda v, j: move(v, dy=j))

    def scatter_zh(values_in):
        return scatter_blocks(values_in, n_zh, lambda v, j: move(v, dzh=j))

    def scatter_t(values_in):
        return scatter_zh(scatter_y(values_in))

    def gather_group(values_in):
        return join_cores(gather_near(values_in))

    slots = jnp.arange(n_dev, dtype=jnp.int32)

    def device_of(part_core, part_zx, part_t):
        part_zh, part_y = part_t % n_zh, part_t // n_zh
        slot_dp = (zh ^ part_zh) * 4 + (part_zx // 2) * 2 + part_core
        return slot_dp * n_ctx + (y ^ part_y) * 2 + part_zx % 2

    dev_all = device_of(core ^ (slots // (4 * n_t)), zx ^ ((slots // n_t) % 4), slots % n_t)
    dev_ffn = device_of(slots % 2, (slots // 2) % 4, slots // 8)

    def one_hot(total, rows, slot_dev, padded):
        inner = jnp.arange(padded, dtype=jnp.int32)[None, :]
        natural = jnp.where(inner < rows, slot_dev[:, None] * rows + inner, -1)
        picks = jnp.arange(total, dtype=jnp.int32)[:, None] == natural.reshape(1, -1)
        return picks.astype(BF16)

    rows_w = w_query.shape[0]
    rows_o = w_out.shape[0]
    rows_q = gain_query.shape[0]
    hot_w = one_hot(width, rows_w, dev_all, rows_w)
    hot_o = one_hot(QW, rows_o, dev_all, rows_w)
    hot_f = one_hot(width, rows_w, dev_ffn, rows_w)
    hot_q = one_hot(HD, rows_q, dev_all, rows_w)

    def column(gain):
        return jnp.pad(gain, (0, rows_w - gain.shape[0]))[:, None]

    gain_cols = jnp.concatenate(
        [
            column(g)
            for g in (gain_in, gain_attn_post, gain_ffn_pre, gain_ffn_post, gain_query, gain_key)
        ],
        axis=1,
    )
    w_rows = jnp.concatenate([w_query, w_key, w_value], axis=1)
    n_qkv = w_rows.shape[1]
    n_wide = n_qkv + 128
    payload = jnp.concatenate(
        [
            w_rows,
            jnp.pad(gain_cols, ((0, 0), (0, 128 - 6))),
            jnp.pad(w_out, ((0, rows_w - rows_o), (0, 0))),
        ],
        axis=1,
    )
    payload_zh = gather_zh(payload)
    payload_t = gather_y(payload_zh)
    near_qkv = gather_near(payload_t[:, :n_wide])
    full_w = join_cores(near_qkv)
    full_qkv = full_w[:, :n_qkv]
    full_gains = full_w[:, n_qkv:]
    gains_d = jnp.einsum("kg,dk->gd", full_gains, hot_w, preferred_element_type=F32)
    gains_h = jnp.einsum("kg,dk->gd", full_gains, hot_q, preferred_element_type=F32)
    norm_in, norm_attn_post, norm_ffn_pre, norm_ffn_post = (gains_d[i] for i in range(4))
    norm_query, norm_key = gains_h[4], gains_h[5]
    near_out = gather_near(after(payload_t[:, n_wide:], *near_qkv))

    units = w_down.shape[0]
    cols = n_t * units

    blocks = split_columns(w_gate, w_up, core, n_t, n_y, units)
    kept = blocks[0]
    got = move(blocks[1], dcore=1)
    paired = jnp.where(
        core == 0, jnp.concatenate([kept, got], axis=2), jnp.concatenate([got, kept], axis=2)
    )
    group_rows = jnp.zeros((2, 4, 2 * rows_w, cols), BF16)
    for k in range(4):
        piece = pick(paired, zx ^ k)
        group_rows = put(group_rows, near(piece, k) if k else piece, zx ^ k, 1)
    group_rows = group_rows.reshape(2, 8 * rows_w, cols)

    down_line = [w_down] + [move(after(w_down, payload_zh), dzh=j) for j in range(1, n_zh)]
    near_line = [after(p, *near_qkv) for p in down_line[1:]]
    down_parts = [
        [after(w_down, payload_t) if j else w_down] + near_line for j in range(n_y)
    ]
    down_parts = [
        [move(p, dy=j) if j else down_line[i] for i, p in enumerate(line)]
        for j, line in enumerate(down_parts)
    ]

    def join_down(held_by):
        joined = jnp.zeros((n_zh, n_y, units, width), BF16)
        for j in range(n_y):
            for i in range(n_zh):
                part = after(down_parts[j][i], held_by)[None, None]
                joined = lax.dynamic_update_slice(joined, part, (zh ^ i, y ^ j, 0, 0))
        return joined.reshape(cols, width)

    far_zh = [[move(group_rows[i], dzh=j) for j in range(1, n_zh)] for i in range(2)]
    far_y = [move(group_rows, dy=j) for j in range(1, n_y)]

    def join_groups(i, came_zh):
        parts = [group_rows[i]] + came_zh
        for j in range(1, n_y):
            parts = parts + [far_y[j - 1][i]] + [move(p, dy=j) for p in came_zh]
        return jnp.concatenate(parts, axis=0)

    seq_lengths = lengths[0]
    inner = jnp.arange(tok_dev, dtype=jnp.int32)
    local_places = places_of(jnp.full_like(inner, ctx), inner, tok_dev, n_ctx)
    row_owner = ctx ^ jnp.arange(n_ctx, dtype=jnp.int32)
    row_places = places_of(row_owner[:, None], inner[None, :], tok_dev, n_ctx).reshape(-1)
    local_segment, local_relative = segment_info(local_places, seq_lengths)
    row_segment, row_relative = segment_info(row_places, seq_lengths)
    cosine, sine = rope_tables(local_relative)

    def swap_c(values_in, j):
        return move(values_in, dy=j // 2, dx=j % 2)

    def query_piece(query_lin, gain):
        shaped = query_lin.reshape(tok_dev, HEADS, HD)
        return rotate(rms_norm(shaped, gain), cosine[:, None, :], sine[:, None, :])

    def key_piece(key_lin, gain):
        return rotate(rms_norm(key_lin, gain), cosine, sine)

    layer_in = tokens.astype(F32)
    normed, pull_in = jax.vjp(lambda v: rms_norm(v, norm_in), layer_in)
    normed_slots = matmul_fast(normed.astype(BF16), hot_w).astype(BF16)
    qkv_lin = matmul_fast(normed_slots, full_qkv)
    query_lin = qkv_lin[:, :QW]
    key_lin = qkv_lin[:, QW : QW + HD]
    value_lin = qkv_lin[:, QW + HD :]
    query_rot, pull_query = jax.vjp(query_piece, query_lin, norm_query)
    key_rot, pull_key = jax.vjp(key_piece, key_lin, norm_key)
    query_low = query_rot.astype(BF16).reshape(tok_dev * HEADS, HD)
    own_kv = jnp.concatenate([key_rot.astype(BF16), value_lin.astype(BF16)], axis=1)
    row_kv = jnp.concatenate([own_kv] + [swap_c(own_kv, j) for j in range(1, n_ctx)], axis=0)
    row_keys = row_kv[:, :HD]
    row_values = row_kv[:, HD:]
    query_segment = jnp.repeat(local_segment, HEADS)
    query_places = jnp.repeat(local_places, HEADS)
    allowed = (query_segment[:, None] == row_segment[None, :]) & (
        row_places[None, :] <= query_places[:, None]
    )
    gate_zh = [after(p, query_low) for p in far_zh[0]]
    full_out = join_cores([after(p, query_low) for p in near_out])
    raw = right_transposed(query_low, row_keys) * scale
    scores = jnp.where(allowed, raw, MASKED_SCORE)
    row_max = jnp.max(scores, axis=-1, keepdims=True)
    expo = jnp.exp(scores - row_max)
    total = jnp.sum(expo, axis=-1, keepdims=True)
    probs = expo / total
    probs_low = probs.astype(BF16)
    attended = matmul_fast(after(probs_low, *gate_zh), row_values)
    attended_low = attended.astype(BF16).reshape(tok_dev, QW)
    attended_slots = matmul_fast(attended_low, hot_o).astype(BF16)
    up_zh = [after(p, attended_slots) for p in far_zh[1]]
    branch_attn = matmul_fast(after(attended_slots, *up_zh), full_out)
    post_attn, pull_attn_post = jax.vjp(rms_norm, branch_attn, norm_attn_post)
    hidden_one = layer_in + post_attn
    ffn_in, pull_ffn_pre = jax.vjp(rms_norm, hidden_one, norm_ffn_pre)

    half = 4 * tok_dev

    def scatter_group(left, right):
        far = right(left[half:]).astype(BF16)
        total = low_sum(right(left[:half]), move(far, dcore=1))
        return scatter_blocks(total, 4, near)

    ffn_source = gather_group(matmul_fast(ffn_in.astype(BF16), hot_f).astype(BF16))
    full_gate = join_groups(0, gate_zh)
    full_up = join_groups(1, up_zh)
    full_down = join_down(ffn_source)
    gate = matmul_fast(ffn_source, full_gate)
    upward = matmul_fast(ffn_source, full_up)
    hidden, pull_ffn = jax.vjp(ffn_piece, gate, upward)
    hidden_low = hidden.astype(BF16)
    branch_ffn = scatter_group(hidden_low, lambda v: matmul_fast(v, full_down))
    post_ffn, pull_ffn_post = jax.vjp(rms_norm, branch_ffn, norm_ffn_post)
    layer_out = (hidden_one + post_ffn).astype(BF16)

    grad_out = cotangent.astype(F32)
    grad_branch_ffn, grad_ffn_post = pull_ffn_post(grad_out)
    grad_branch_rows = gather_group(grad_branch_ffn.astype(BF16))
    grad_hidden = right_transposed(grad_branch_rows, full_down)
    grad_gate, grad_upward = pull_ffn(grad_hidden)
    grad_gate_low = grad_gate.astype(BF16)
    grad_up_low = grad_upward.astype(BF16)

    def grad_terms(part):
        return right_transposed(grad_gate_low[part], full_gate) + right_transposed(
            grad_up_low[part], full_up
        )

    grad_far = move(grad_terms(slice(half, None)).astype(BF16), dcore=1)
    grad_chip = low_sum(grad_terms(slice(None, half)), grad_far)
    grad_ffn_slots = scatter_blocks(grad_chip, 4, near)
    grad_ffn_in = right_transposed(grad_ffn_slots.astype(BF16), hot_f)
    held = after(ffn_source, grad_chip)
    rows_first = Layout(major_to_minor=(0, 1))
    grad_w_gate = with_layout_constraint(left_transposed(held, grad_gate_low), rows_first)
    grad_w_up = with_layout_constraint(left_transposed(held, grad_up_low), rows_first)
    grad_down = left_transposed(after(hidden_low, grad_chip), grad_branch_rows)
    grad_down = grad_down.reshape(n_zh, n_y, units, width)

    grad_hidden_part, grad_ffn_pre = pull_ffn_pre(grad_ffn_in)
    grad_hidden_one = grad_out + grad_hidden_part
    grad_branch_attn, grad_attn_post = pull_attn_post(grad_hidden_one)
    grad_attn_low = grad_branch_attn.astype(BF16)
    grad_out_w = left_transposed(attended_slots, grad_attn_low)
    out_chip = scatter_blocks(grad_out_w, 2, lambda v, j: move(v, dcore=j))
    grad_attended_slots = right_transposed(grad_attn_low, full_out).astype(BF16)
    grad_attended_low = right_transposed(grad_attended_slots, hot_o).astype(BF16)
    grad_attended_low = grad_attended_low.reshape(tok_dev * HEADS, HD)
    grad_probs = right_transposed(grad_attended_low, row_values)
    delta = jnp.sum(grad_probs * probs, axis=-1, keepdims=True)
    grad_scores_low = (probs * (grad_probs - delta)).astype(BF16)
    key_part = left_transposed(grad_scores_low, query_low) * scale
    value_part = left_transposed(probs_low, grad_attended_low)
    kv_part = jnp.concatenate([key_part, value_part], axis=1)
    grad_kv = scatter_blocks(kv_part, n_ctx, swap_c)
    grad_query_rows = matmul_fast(grad_scores_low, row_keys) * scale
    grad_query_lin, grad_norm_query = pull_query(grad_query_rows.reshape(tok_dev, HEADS, HD))
    grad_key_lin, grad_norm_key = pull_key(grad_kv[:, :HD])
    grad_qkv_low = jnp.concatenate(
        [grad_query_lin, grad_key_lin, grad_kv[:, HD:]], axis=1
    ).astype(BF16)
    out_near = scatter_blocks(after(out_chip, kv_part), 4, near)
    gate_y = scatter_blocks(grad_w_gate, n_y, lambda v, j: after(move(v, dy=j), kv_part))
    up_y = scatter_blocks(
        grad_w_up, n_y, lambda v, j: after(move(after(v, grad_kv), dy=j), grad_qkv_low)
    )
    grad_qkv_low = after(grad_qkv_low, gate_y)
    grad_qkv_w = left_transposed(normed_slots, grad_qkv_low)
    grads_d = jnp.stack([grad_attn_post, grad_ffn_pre, grad_ffn_post]).astype(BF16)
    grads_h = jnp.stack([grad_norm_query, grad_norm_key]).astype(BF16)
    grad_cols = jnp.concatenate(
        [
            jnp.einsum("dk,gd->kg", hot_w, grads_d, preferred_element_type=F32),
            jnp.einsum("dk,gd->kg", hot_q, grads_h, preferred_element_type=F32),
        ],
        axis=1,
    )
    grad_payload = jnp.concatenate([grad_qkv_w, jnp.pad(grad_cols, ((0, 0), (0, 128 - 5)))], axis=1)
    chip_w = scatter_blocks(grad_payload, 2, lambda v, j: move(v, dcore=j))
    near_w = scatter_blocks(chip_w, 4, near)
    mine_w = scatter_t(jnp.concatenate([near_w, out_near], axis=1))
    out_w_out = mine_w[:rows_o, n_wide:]

    sums = [
        scatter_blocks(v, n_zh, lambda v, j: after(move(v, dzh=j), near_w)) for v in (gate_y, up_y)
    ]
    sums = jnp.stack([v.astype(BF16).reshape(4, 2, rows_w, cols) for v in sums], axis=1)
    owned = jnp.stack([near(pick(sums, zx ^ k), k) if k else pick(sums, zx) for k in range(4)])
    mine = pick(owned, core, 2)
    other = move(pick(owned, 1 - core, 2), dcore=1)
    out_gate, out_up = join_columns(mine, other, zx, core, n_t, n_y, units)
    down_y = pick(grad_down, y, 1)
    for j in range(1, n_y):
        sent = after(pick(grad_down, y ^ j, 1).astype(BF16), grad_qkv_low)
        down_y = low_sum(down_y, after(move(sent, dy=j), near_w))
    out_down = pick(down_y, zh)
    for j in range(1, n_zh):
        out_down = low_sum(out_down, move(pick(down_y, zh ^ j).astype(BF16), dzh=j))
    grad_normed = right_transposed(
        right_transposed(grad_qkv_low, full_qkv).astype(BF16), hot_w
    )
    (grad_in_part,) = pull_in(grad_normed)
    input_grad = (grad_hidden_one + grad_in_part).astype(BF16)
    out_gain_in = jnp.sum(w_rows.astype(F32) * mine_w[:, :n_qkv], axis=1) / gain_in.astype(F32)
    gain_out = mine_w[:, n_qkv:n_wide]
    return (
        layer_out,
        input_grad,
        mine_w[:, :QW],
        mine_w[:, QW : QW + HD],
        mine_w[:, QW + HD : n_qkv],
        out_w_out,
        out_gate,
        out_up,
        out_down,
        out_gain_in,
        gain_out[:, 0],
        gain_out[:, 1],
        gain_out[:, 2],
        gain_out[:rows_q, 3],
        gain_out[:rows_q, 4],
    )


def solution(mesh):
    split = P(("dp", "ctx"), None)
    split_1d = P(("dp", "ctx"))
    in_specs = (split, P("dp", None)) + (split,) * 7 + (split_1d,) * 6 + (split,)
    out_specs = (split,) * 9 + (split_1d,) * 6
    return jax.shard_map(body, mesh=mesh, in_specs=in_specs, out_specs=out_specs, check_vma=False)
```

```python
import jax
import jax.numpy as jnp
from jax import lax
from jax.experimental import pallas as pl
from jax.experimental.layout import Layout, with_layout_constraint
from jax.experimental.pallas import tpu as pltpu
from jax.sharding import PartitionSpec as P

HEADS = 4
HD = 256
QW = HEADS * HD


NORM_EPS = 1e-06
ROPE_BASE = 1000000.0
MASKED_SCORE = -1e30
F32 = jnp.float32
BF16 = jnp.bfloat16


def rms_norm(values_in, gain):
    return (
        values_in
        * lax.rsqrt(jnp.mean(values_in * values_in, axis=-1, keepdims=True) + NORM_EPS)
        * gain
    )


def places_of(owner, inner, tok_dev, n_ctx):
    half_len = tok_dev // 2
    block_id = jnp.where(inner < half_len, owner, 2 * n_ctx - 1 - owner)
    return block_id * half_len + inner % half_len


def segment_info(places, seq_lengths):
    ends = jnp.cumsum(seq_lengths)
    passed = places[:, None] >= ends[None, :]
    segment = jnp.sum(passed.astype(jnp.int32), axis=-1)
    start = jnp.sum(jnp.where(passed, seq_lengths[None, :], 0), axis=-1)
    return (segment, places - start)


def rope_tables(relative):
    head_half = HD // 2
    freqs = ROPE_BASE ** (-(jnp.arange(head_half, dtype=F32) * 2.0 / HD))
    angles = relative.astype(F32)[:, None] * freqs[None, :]
    cosine = jnp.concatenate([jnp.cos(angles), jnp.cos(angles)], axis=-1)
    sine = jnp.concatenate([jnp.sin(angles), jnp.sin(angles)], axis=-1)
    return (cosine, sine)


def rotate(values_in, cosine, sine):
    head_half = values_in.shape[-1] // 2
    turned = jnp.concatenate([-values_in[..., head_half:], values_in[..., :head_half]], axis=-1)
    return values_in * cosine + turned * sine


def ffn_piece(gate, upward):
    return jax.nn.gelu(gate, approximate=True) * upward


def matmul_fast(left, right):
    return jnp.dot(left, right, preferred_element_type=F32)


def left_transposed(left, right):
    return jnp.einsum("ta,tb->ab", left, right, preferred_element_type=F32)


def right_transposed(left, right):
    return jnp.einsum("ta,ba->tb", left, right, preferred_element_type=F32)


def dot(left, right, left_dim, right_dim):
    return lax.dot_general(
        left, right, (((left_dim,), (right_dim,)), ((), ())), preferred_element_type=F32
    )


def inverse_rms(values_in):
    return lax.rsqrt(jnp.mean(values_in * values_in, axis=-1, keepdims=True) + NORM_EPS)


def norm_back(values_in, gain, grad):
    inverse = inverse_rms(values_in)
    unit = values_in * inverse
    scaled = grad * gain
    grad_in = inverse * (scaled - unit * jnp.mean(scaled * unit, axis=-1, keepdims=True))
    return grad_in, jnp.sum(grad * unit, axis=0, keepdims=True)


def rotate_back(grad, cosine, sine):
    half = grad.shape[-1] // 2
    turned = grad * sine
    return grad * cosine + jnp.concatenate([turned[:, half:], -turned[:, :half]], axis=-1)


def head(h):
    return slice(h * HD, (h + 1) * HD)


def on_chip(kernel, out_shape, *operands):
    vmem = pl.BlockSpec(memory_space=pltpu.VMEM)
    return pl.pallas_call(
        kernel,
        out_shape=out_shape,
        in_specs=[vmem] * len(operands),
        out_specs=jax.tree.map(lambda _: vmem, out_shape),
        name=kernel.__name__,
    )(*operands)


def shaped(rows, columns, dtype):
    return jax.ShapeDtypeStruct((rows, columns), dtype)


def project_kernel(tok, w, hot, hot_q, cosine, sine, slots, query, kv, lin, gains, gains_h):
    n_qkv = QW + 2 * HD
    gain_rows = w[:, n_qkv:]
    all_gains = dot(gain_rows, hot[...], 0, 1)
    all_gains_h = dot(gain_rows, hot_q[...], 0, 1)
    gains[...] = all_gains[:8]
    gains_h[...] = all_gains_h[:8]
    layer_in = tok[...].astype(F32)
    normed = (layer_in * inverse_rms(layer_in) * all_gains[0:1]).astype(BF16)
    normed_slots = dot(normed, hot[...], 1, 0).astype(BF16)
    slots[...] = normed_slots
    qkv = dot(normed_slots, w[:, :n_qkv], 1, 0)
    lin[...] = qkv[:, : QW + HD]
    rows = tok.shape[0]

    def turned(values_in, gain):
        return rotate(values_in * inverse_rms(values_in) * gain, cosine[...], sine[...])

    for h in range(HEADS):
        query[h * rows : (h + 1) * rows, :] = turned(qkv[:, head(h)], all_gains_h[4:5]).astype(BF16)
    kv[:, :HD] = turned(qkv[:, head(HEADS)], all_gains_h[5:6]).astype(BF16)
    kv[:, HD:] = qkv[:, head(HEADS + 1)].astype(BF16)


def attend_kernel(
    query, kv, allowed, hot_o, w, tok, gains, hot_f, probs, out_slots, branch, hidden_one, ffn_slots
):
    rows = tok.shape[0]
    mask = allowed[...] > 0
    total = jnp.zeros(out_slots.shape, F32)
    for h in range(HEADS):
        part = slice(h * rows, (h + 1) * rows)
        raw = dot(query[part, :], kv[:, :HD], 1, 1) * HD ** (-0.5)
        scores = jnp.where(mask, raw, MASKED_SCORE)
        expo = jnp.exp(scores - jnp.max(scores, axis=-1, keepdims=True))
        prob = expo / jnp.sum(expo, axis=-1, keepdims=True)
        probs[part, :] = prob
        attended = dot(prob.astype(BF16), kv[:, HD:], 1, 0).astype(BF16)
        total += dot(attended, hot_o[head(h), :], 1, 0)
    total = total.astype(BF16)
    out_slots[...] = total
    y = dot(total, w[:, QW + 2 * HD + 128 :], 1, 0)
    branch[...] = y
    one = tok[...].astype(F32) + y * inverse_rms(y) * gains[1:2, :]
    hidden_one[...] = one
    ffn_in = (one * inverse_rms(one) * gains[2:3, :]).astype(BF16)
    ffn_slots[...] = dot(ffn_in, hot_f[...], 1, 0).astype(BF16)


def attend_back_kernel(
    grad_slots, hot_f, hidden_one, branch, cotangent, gains, gains_h, w, hot_o,
    query, kv, probs, lin, cosine, sine,
    grad_one, grad_gains, grad_query_gain, grad_branch, kv_part, grad_lin,
):
    rows = cotangent.shape[0]
    grad_in = dot(grad_slots[...].astype(BF16), hot_f[...], 1, 1)
    part, gain_pre = norm_back(hidden_one[...], gains[2:3, :], grad_in)
    one = cotangent[...].astype(F32) + part
    grad_one[...] = one
    grad_y, gain_post = norm_back(branch[...], gains[1:2, :], one)
    grad_gains[...] = jnp.concatenate(
        [gain_post, gain_pre, jnp.zeros((6, gain_pre.shape[1]), F32)], axis=0
    )
    grad_y = grad_y.astype(BF16)
    grad_branch[...] = grad_y
    grad_slots_o = dot(grad_y, w[:, QW + 2 * HD + 128 :], 1, 1).astype(BF16)
    keys, values = kv[:, :HD], kv[:, HD:]
    grad_keys = jnp.zeros(keys.shape, F32)
    grad_values = jnp.zeros(values.shape, F32)
    gain_sum = jnp.zeros((1, HD), F32)
    for h in range(HEADS):
        span = slice(h * rows, (h + 1) * rows)
        grad_o = dot(grad_slots_o, hot_o[head(h), :], 1, 1).astype(BF16)
        prob = probs[span, :]
        grad_prob = dot(grad_o, values, 1, 1)
        delta = jnp.sum(grad_prob * prob, axis=-1, keepdims=True)
        grad_score = (prob * (grad_prob - delta)).astype(BF16)
        grad_keys += dot(grad_score, query[span, :], 0, 0)
        grad_values += dot(prob.astype(BF16), grad_o, 0, 0)
        grad_query = rotate_back(
            dot(grad_score, keys, 1, 0) * HD ** (-0.5), cosine[...], sine[...]
        )
        grad_head, gain = norm_back(lin[:, head(h)], gains_h[4:5, :], grad_query)
        gain_sum += gain
        grad_lin[:, head(h)] = grad_head.astype(BF16)
    kv_part[:, :HD] = grad_keys * HD ** (-0.5)
    kv_part[:, HD:] = grad_values
    grad_query_gain[...] = jnp.concatenate([gain_sum, jnp.zeros((7, HD), F32)], axis=0)


def project_back_kernel(
    grad_kv, lin, gains_h, cosine, sine, grad_query_lin, slots, hot, hot_q, grad_gains,
    grad_ffn_post, grad_query_gain, grad_lin, mine, sent,
):
    half = mine.shape[0]
    n_qkv = QW + 2 * HD
    grad_key, gain_key = norm_back(
        lin[...], gains_h[5:6, :], rotate_back(grad_kv[:, :HD], cosine[...], sine[...])
    )
    grad_lin[:, :QW] = grad_query_lin[...]
    grad_lin[:, head(HEADS)] = grad_key.astype(BF16)
    grad_lin[:, head(HEADS + 1)] = grad_kv[:, HD:].astype(BF16)
    grad_w = dot(slots[...], grad_lin[...], 0, 0)
    mine[:, :n_qkv] = grad_w[:half]
    sent[:, :n_qkv] = grad_w[half:].astype(BF16)
    wide = jnp.concatenate(
        [grad_gains[0:2, :], grad_ffn_post[...], jnp.zeros((125, hot.shape[0]), F32)], axis=0
    )
    narrow = jnp.concatenate(
        [jnp.zeros((3, HD), F32), grad_query_gain[0:1, :], gain_key, jnp.zeros((123, HD), F32)], axis=0
    )
    columns = dot(hot[...], wide.astype(BF16), 0, 1) + dot(hot_q[...], narrow.astype(BF16), 0, 1)
    mine[:, n_qkv:] = columns[:half]
    sent[:, n_qkv:] = columns[half:].astype(BF16)


def device_columns(k, c, t, n_y, units):
    start = (((t // n_y) * 4 + (k // 2) * 2 + c) * 2 * n_y + (t % n_y) * 2 + k % 2) * units
    return slice(start, start + units)


def split_columns(w_gate, w_up, core, n_t, n_y, units):
    rows = w_gate.shape[0]

    def kernel(core_ref, gate_ref, up_ref, out_ref):
        own = core_ref[0]
        for i, ref in enumerate((gate_ref, up_ref)):
            for c in range(2):
                for k in range(4):
                    for t in range(n_t):
                        out_ref[own ^ c, k, i, :, t * units : (t + 1) * units] = ref[
                            :, device_columns(k, c, t, n_y, units)
                        ]

    vmem = pl.BlockSpec(memory_space=pltpu.VMEM)
    return pl.pallas_call(
        kernel,
        out_shape=jax.ShapeDtypeStruct((2, 4, 2, rows, n_t * units), BF16),
        in_specs=[pl.BlockSpec(memory_space=pltpu.SMEM), vmem, vmem],
        out_specs=vmem,
        name="split_columns",
    )(jnp.reshape(core, (1,)), w_gate, w_up)


def join_columns(mine, other, zx, core, n_t, n_y, units):
    rows = mine.shape[2]

    def kernel(place_ref, mine_ref, other_ref, *outs):
        for i, out_ref in enumerate(outs):
            for k in range(4):
                own_core = mine_ref[place_ref[0] ^ k, i].astype(F32)
                other_core = other_ref[place_ref[0] ^ k, i].astype(F32)
                for c in range(2):
                    found = jnp.where(place_ref[1] == c, own_core, other_core)
                    for t in range(n_t):
                        out_ref[:, device_columns(k, c, t, n_y, units)] = found[
                            :, t * units : (t + 1) * units
                        ]

    vmem = pl.BlockSpec(memory_space=pltpu.VMEM)
    out = jax.ShapeDtypeStruct((rows, 8 * n_t * units), F32)
    return pl.pallas_call(
        kernel,
        out_shape=(out, out),
        in_specs=[pl.BlockSpec(memory_space=pltpu.SMEM), vmem, vmem],
        out_specs=(vmem, vmem),
        name="join_columns",
    )(jnp.stack([zx, core]), mine, other)


def body(
    tokens,
    lengths,
    w_query,
    w_key,
    w_value,
    w_out,
    w_gate,
    w_up,
    w_down,
    gain_in,
    gain_attn_post,
    gain_ffn_pre,
    gain_ffn_post,
    gain_query,
    gain_key,
    cotangent,
):
    n_ctx = lax.axis_size("ctx")
    n_dp = lax.axis_size("dp")
    n_y = n_ctx // 2
    n_zh = n_dp // 4
    n_t = n_y * n_zh
    n_dev = n_dp * n_ctx
    tok_dev, width = tokens.shape
    dp = lax.axis_index("dp")
    ctx = lax.axis_index("ctx")
    zh, zl, core = dp // 4, (dp // 2) % 2, dp % 2
    y, x = ctx // 2, ctx % 2
    zx = zl * 2 + x

    def move(values_in, dzh=0, dzl=0, dcore=0, dy=0, dx=0):
        pairs = [
            (d * n_ctx + c, (d ^ (4 * dzh + 2 * dzl + dcore)) * n_ctx + (c ^ (2 * dy + dx)))
            for d in range(n_dp)
            for c in range(n_ctx)
        ]
        return lax.ppermute(values_in, ("dp", "ctx"), pairs)

    def near(values_in, k):
        return move(values_in, dzl=k // 2, dx=k % 2)

    def pick(values_in, index, axis=0):
        return lax.dynamic_index_in_dim(values_in, index, axis, keepdims=False)

    def put(buffer, values_in, index, axis=0):
        return lax.dynamic_update_index_in_dim(buffer, values_in, index, axis)

    def after(values_in, *others):
        return lax.optimization_barrier((values_in,) + others)[0]

    def gather_zh(rows):
        return after(
            jnp.concatenate([rows] + [move(rows, dzh=j) for j in range(1, n_zh)], axis=0)
        )

    def gather_y(rows):
        return after(jnp.concatenate([rows] + [move(rows, dy=j) for j in range(1, n_y)], axis=0))

    def gather_near(rows):
        return [rows] + [near(rows, k) for k in range(1, 4)]

    def join_cores(own):
        return jnp.concatenate(own + [move(p, dcore=1) for p in own], axis=0)

    def low_sum(total, got):
        return total + got.astype(F32)

    def scatter_blocks(values_in, n, send):
        rows = values_in.shape[0] // n
        total = values_in[:rows]
        for j in range(1, n):
            total = low_sum(total, send(values_in[j * rows : (j + 1) * rows].astype(BF16), j))
        return total

    def scatter_halves(values_in):
        rows = values_in.shape[0] // 4
        low = values_in.astype(BF16)
        sent = jnp.concatenate([low[rows : 2 * rows], low[3 * rows :]], axis=0)
        came = move(sent, dx=1)
        total = low_sum(values_in[:rows], came[:rows])
        passed = low_sum(values_in[2 * rows : 3 * rows], came[rows:])
        return low_sum(total, move(passed.astype(BF16), dzl=1))

    def scatter_y(values_in):
        return scatter_blocks(values_in, n_y, lambda v, j: move(v, dy=j))

    def scatter_zh(values_in):
        return scatter_blocks(values_in, n_zh, lambda v, j: move(v, dzh=j))

    def scatter_t(values_in):
        return scatter_zh(scatter_y(values_in))

    def gather_group(values_in):
        return join_cores(gather_near(values_in))

    rows_w = w_query.shape[0]
    rows_o = w_out.shape[0]
    rows_q = gain_query.shape[0]

    def column(gain):
        return jnp.pad(gain, (0, rows_w - gain.shape[0]))[:, None]

    gain_cols = jnp.concatenate(
        [
            column(g)
            for g in (gain_in, gain_attn_post, gain_ffn_pre, gain_ffn_post, gain_query, gain_key)
        ],
        axis=1,
    )
    w_rows = jnp.concatenate([w_query, w_key, w_value], axis=1)
    n_qkv = w_rows.shape[1]
    n_wide = n_qkv + 128
    payload = jnp.concatenate(
        [
            w_rows,
            jnp.pad(gain_cols, ((0, 0), (0, 128 - 6))),
            jnp.pad(w_out, ((0, rows_w - rows_o), (0, 0))),
        ],
        axis=1,
    )
    payload_zh = gather_zh(payload)
    payload_t = gather_y(payload_zh)

    slots = after(jnp.arange(n_dev, dtype=jnp.int32), payload_zh)

    def device_of(part_core, part_zx, part_t):
        part_zh, part_y = part_t % n_zh, part_t // n_zh
        slot_dp = (zh ^ part_zh) * 4 + (part_zx // 2) * 2 + part_core
        return slot_dp * n_ctx + (y ^ part_y) * 2 + part_zx % 2

    dev_all = device_of(core ^ (slots // (4 * n_t)), zx ^ ((slots // n_t) % 4), slots % n_t)
    dev_ffn = device_of(slots % 2, (slots // 2) % 4, slots // 8)

    def one_hot(total, rows, slot_dev, padded):
        inner = jnp.arange(padded, dtype=jnp.int32)[None, :]
        natural = jnp.where(inner < rows, slot_dev[:, None] * rows + inner, -1)
        picks = jnp.arange(total, dtype=jnp.int32)[:, None] == natural.reshape(1, -1)
        return picks.astype(BF16)

    hot_w = one_hot(width, rows_w, dev_all, rows_w)
    hot_q = one_hot(HD, rows_q, dev_all, rows_w)
    hot_o = one_hot(QW, rows_o, dev_all, rows_w)
    half_w = width // 2
    hot_o = after(hot_o)
    hot_f = one_hot(width, rows_w, dev_ffn, rows_w)
    hot_w, hot_f, hot_q = after((hot_w, hot_f, hot_q))

    down_own_y = [move(after(w_down, payload_t), dy=j) for j in range(1, n_y)]
    near_w = [payload_t, move(payload_t, dx=1), move(payload_t, dzl=1)]
    near_w.append(move(near_w[2], dx=1))
    down_zh = [move(after(w_down, payload_zh), dzh=j) for j in range(1, n_zh)]
    near_w[1] = after(near_w[1], *down_zh)
    near_w[3] = after(near_w[3], *down_own_y)
    full_w = join_cores(near_w)

    units = w_down.shape[0]
    cols = n_t * units

    blocks = split_columns(w_gate, w_up, core, n_t, n_y, units)
    kept = blocks[0]
    got = move(blocks[1], dcore=1)
    paired = jnp.where(
        core == 0, jnp.concatenate([kept, got], axis=2), jnp.concatenate([got, kept], axis=2)
    )
    group_rows = jnp.zeros((2, 4, 2 * rows_w, cols), BF16)
    for k in range(4):
        piece = pick(paired, zx ^ k)
        group_rows = put(group_rows, near(piece, k) if k else piece, zx ^ k, 1)
    group_rows = group_rows.reshape(2, 8 * rows_w, cols)

    down_zh = [after(p, full_w) for p in down_zh]

    def join_down(held_by, down_far):
        joined = jnp.zeros((n_zh, n_y, units, width), BF16)
        for j in range(n_y):
            line = [down_own_y[j - 1]] + down_far[j - 1] if j else [w_down] + down_zh
            for i in range(n_zh):
                part = after(line[i], held_by)[None, None]
                joined = lax.dynamic_update_slice(joined, part, (zh ^ i, y ^ j, 0, 0))
        return joined.reshape(cols, width)

    gate_zh = [move(group_rows[0], dzh=j) for j in range(1, n_zh)]
    up_zh = [move(group_rows[1], dzh=j) for j in range(1, n_zh)]
    full_w = after(full_w, *gate_zh)
    full_qkv = full_w[:, :n_qkv]
    gate_far = [[move(p, dy=j) for p in gate_zh] for j in range(1, n_y)]
    wide_y = [move(group_rows, dy=j) for j in range(1, n_y)]

    def join_groups(i, came_zh, far):
        parts = [group_rows[i]] + came_zh
        for own, forwarded in zip(wide_y, far):
            parts = parts + [own[i]] + forwarded
        return jnp.concatenate(parts, axis=0)

    seq_lengths = lengths[0]
    inner = jnp.arange(tok_dev, dtype=jnp.int32)
    local_places = places_of(jnp.full_like(inner, ctx), inner, tok_dev, n_ctx)
    row_owner = ctx ^ jnp.arange(n_ctx, dtype=jnp.int32)
    row_places = places_of(row_owner[:, None], inner[None, :], tok_dev, n_ctx).reshape(-1)
    local_segment, local_relative = segment_info(local_places, seq_lengths)
    row_segment, row_relative = segment_info(row_places, seq_lengths)
    cosine, sine = rope_tables(local_relative)

    def swap_c(values_in, j):
        return move(values_in, dy=j // 2, dx=j % 2)

    layer_in = tokens.astype(F32)
    row_len = n_ctx * tok_dev
    normed_slots, query_low, own_kv, qk_lin, gains, gains_h = on_chip(
        project_kernel,
        (
            shaped(tok_dev, width, BF16),
            shaped(HEADS * tok_dev, HD, BF16),
            shaped(tok_dev, 2 * HD, BF16),
            shaped(tok_dev, QW + HD, F32),
            shaped(8, width, F32),
            shaped(8, HD, F32),
        ),
        tokens, after(full_w, *wide_y), hot_w, hot_q, cosine, sine,
    )
    row_kv = jnp.concatenate([own_kv] + [swap_c(own_kv, j) for j in range(1, n_ctx)], axis=0)
    up_zh = [after(p, row_kv) for p in up_zh]
    down_far = [[move(after(p, row_kv), dy=j) for p in down_zh] for j in range(1, n_y)]
    allowed = (local_segment[:, None] == row_segment[None, :]) & (
        row_places[None, :] <= local_places[:, None]
    )
    up_far = [[move(p, dy=j) for p in up_zh] for j in range(1, n_y)]
    probs, out_slots, branch_attn, hidden_one, ffn_slots = on_chip(
        attend_kernel,
        (
            shaped(HEADS * tok_dev, row_len, F32),
            shaped(tok_dev, width, BF16),
            shaped(tok_dev, width, F32),
            shaped(tok_dev, width, F32),
            shaped(tok_dev, width, BF16),
        ),
        after(query_low, *up_zh), after(row_kv, *sum(gate_far, [])), allowed.astype(F32), hot_o, full_w,
        tokens, gains, hot_f,
    )

    half = 4 * tok_dev

    def scatter_group(left, right):
        far = right(left[half:]).astype(BF16)
        total = low_sum(right(left[:half]), move(far, dcore=1))
        return scatter_blocks(total, 4, near)

    ffn_source = gather_group(ffn_slots)
    full_gate = join_groups(0, gate_zh, gate_far)
    full_up = join_groups(1, up_zh, up_far)
    gate = matmul_fast(ffn_source, full_gate)
    upward = matmul_fast(ffn_source, full_up)
    full_down = join_down(gate, down_far)
    hidden, pull_ffn = jax.vjp(ffn_piece, gate, upward)
    hidden_low = hidden.astype(BF16)
    branch_ffn = scatter_group(hidden_low, lambda v: matmul_fast(v, full_down))
    post_ffn, pull_ffn_post = jax.vjp(rms_norm, branch_ffn, gains[3])
    layer_out = (hidden_one + post_ffn).astype(BF16)

    grad_out = cotangent.astype(F32)
    grad_branch_ffn, grad_ffn_post = pull_ffn_post(grad_out)
    grad_branch_rows = gather_group(grad_branch_ffn.astype(BF16))
    grad_hidden = right_transposed(grad_branch_rows, full_down)
    grad_gate, grad_upward = pull_ffn(grad_hidden)
    grad_gate_low = grad_gate.astype(BF16)
    grad_up_low = grad_upward.astype(BF16)

    def grad_terms(part):
        return right_transposed(grad_gate_low[part], full_gate) + right_transposed(
            grad_up_low[part], full_up
        )

    grad_far = move(grad_terms(slice(half, None)).astype(BF16), dcore=1)
    grad_chip = low_sum(grad_terms(slice(None, half)), grad_far)
    grad_ffn_slots = scatter_blocks(grad_chip, 4, near)
    held = after(ffn_source, grad_chip)
    rows_first = Layout(major_to_minor=(0, 1))
    grad_w_gate = with_layout_constraint(left_transposed(held, grad_gate_low), rows_first)
    grad_w_up = with_layout_constraint(left_transposed(held, grad_up_low), rows_first)
    grad_down = left_transposed(after(hidden_low, grad_chip), grad_branch_rows)
    grad_down = grad_down.reshape(n_zh, n_y, units, width)

    grad_hidden_one, grad_gains, grad_query_gain, grad_attn_low, kv_part, grad_query_lin = on_chip(
        attend_back_kernel,
        (
            shaped(tok_dev, width, F32),
            shaped(8, width, F32),
            shaped(8, HD, F32),
            shaped(tok_dev, width, BF16),
            shaped(row_len, 2 * HD, F32),
            shaped(tok_dev, QW, BF16),
        ),
        grad_ffn_slots, hot_f, hidden_one, branch_attn, cotangent, gains, gains_h, full_w,
        hot_o, query_low, row_kv, probs, qk_lin, cosine, sine,
    )
    out_chip = scatter_blocks(
        left_transposed(out_slots, grad_attn_low), 2, lambda v, j: move(v, dcore=j)
    )
    out_near = scatter_blocks(out_chip, 4, near)
    rows_y = width // n_y
    gate_came = [
        after(move(grad_w_gate[j * rows_y : (j + 1) * rows_y].astype(BF16), dy=j), grad_query_lin)
        for j in range(1, n_y)
    ]
    grad_kv = scatter_blocks(after(kv_part, *gate_came), n_ctx, swap_c)
    gate_y = grad_w_gate[:rows_y]
    for came in gate_came:
        gate_y = low_sum(gate_y, came)
    grad_qkv_low, chip_mine, chip_sent = on_chip(
        project_back_kernel,
        (
            shaped(tok_dev, n_qkv, BF16),
            shaped(half_w, n_wide, F32),
            shaped(half_w, n_wide, BF16),
        ),
        after(grad_kv, gate_y, out_near), after(qk_lin, kv_part)[:, QW:], gains_h, cosine, sine, grad_query_lin, normed_slots,
        hot_w, hot_q, grad_gains, grad_ffn_post[None, :], grad_query_gain,
    )
    up_y = scatter_blocks(
        grad_w_up, n_y, lambda v, j: after(move(after(v, grad_kv), dy=j), grad_qkv_low)
    )
    gate_sum = scatter_blocks(
        gate_y, n_zh, lambda v, j: after(move(v, dzh=j), chip_sent)
    )
    chip_w = low_sum(chip_mine, move(chip_sent, dcore=1))
    down_y = pick(grad_down, y, 1)
    for j in range(1, n_y):
        sent = after(pick(grad_down, y ^ j, 1).astype(BF16), grad_qkv_low)
        down_y = low_sum(down_y, after(move(sent, dy=j), chip_w))
    near_w = after(scatter_blocks(after(chip_w, up_y), 4, near), down_y)
    mine_w = scatter_t(jnp.concatenate([near_w, out_near], axis=1))
    out_w_out = mine_w[:rows_o, n_wide:]
    sums = [
        gate_sum,
        scatter_blocks(up_y, n_zh, lambda v, j: after(move(v, dzh=j), near_w)),
    ]
    sums = jnp.stack([v.astype(BF16).reshape(4, 2, rows_w, cols) for v in sums], axis=1)
    owned = jnp.stack([near(pick(sums, zx ^ k), k) if k else pick(sums, zx) for k in range(4)])
    mine = pick(owned, core, 2)
    other = move(pick(owned, 1 - core, 2), dcore=1)
    out_gate, out_up = join_columns(mine, other, zx, core, n_t, n_y, units)
    out_down = pick(down_y, zh)
    for j in range(1, n_zh):
        out_down = low_sum(out_down, move(pick(down_y, zh ^ j).astype(BF16), dzh=j))
    grad_normed = right_transposed(
        right_transposed(grad_qkv_low, full_qkv).astype(BF16), hot_w
    )
    grad_in_part, _ = norm_back(layer_in, gains[0], grad_normed)
    input_grad = (grad_hidden_one + grad_in_part).astype(BF16)
    out_gain_in = jnp.sum(w_rows.astype(F32) * mine_w[:, :n_qkv], axis=1) / gain_in.astype(F32)
    gain_out = mine_w[:, n_qkv:n_wide]
    return (
        layer_out,
        input_grad,
        mine_w[:, :QW],
        mine_w[:, QW : QW + HD],
        mine_w[:, QW + HD : n_qkv],
        out_w_out,
        out_gate,
        out_up,
        out_down,
        out_gain_in,
        gain_out[:, 0],
        gain_out[:, 1],
        gain_out[:, 2],
        gain_out[:rows_q, 3],
        gain_out[:rows_q, 4],
    )


def solution(mesh):
    split = P(("dp", "ctx"), None)
    split_1d = P(("dp", "ctx"))
    in_specs = (split, P("dp", None)) + (split,) * 7 + (split_1d,) * 6 + (split,)
    out_specs = (split,) * 9 + (split_1d,) * 6
    return jax.shard_map(body, mesh=mesh, in_specs=in_specs, out_specs=out_specs, check_vma=False)
```

```python
import jax
import jax.numpy as jnp
from jax import lax
from jax.experimental import pallas as pl
from jax.experimental.layout import Layout, with_layout_constraint
from jax.experimental.pallas import tpu as pltpu
from jax.sharding import PartitionSpec as P

HEADS = 4
HD = 256
QW = HEADS * HD


NORM_EPS = 1e-06
ROPE_BASE = 1000000.0
MASKED_SCORE = -1e30
F32 = jnp.float32
BF16 = jnp.bfloat16


def rms_norm(values_in, gain):
    return (
        values_in
        * lax.rsqrt(jnp.mean(values_in * values_in, axis=-1, keepdims=True) + NORM_EPS)
        * gain
    )


def places_of(owner, inner, tok_dev, n_ctx):
    half_len = tok_dev // 2
    block_id = jnp.where(inner < half_len, owner, 2 * n_ctx - 1 - owner)
    return block_id * half_len + inner % half_len


def segment_info(places, seq_lengths):
    ends = jnp.cumsum(seq_lengths)
    passed = places[:, None] >= ends[None, :]
    segment = jnp.sum(passed.astype(jnp.int32), axis=-1)
    start = jnp.sum(jnp.where(passed, seq_lengths[None, :], 0), axis=-1)
    return (segment, places - start)


def rope_tables(relative):
    head_half = HD // 2
    freqs = ROPE_BASE ** (-(jnp.arange(head_half, dtype=F32) * 2.0 / HD))
    angles = relative.astype(F32)[:, None] * freqs[None, :]
    cosine = jnp.concatenate([jnp.cos(angles), jnp.cos(angles)], axis=-1)
    sine = jnp.concatenate([jnp.sin(angles), jnp.sin(angles)], axis=-1)
    return (cosine, sine)


def rotate(values_in, cosine, sine):
    head_half = values_in.shape[-1] // 2
    turned = jnp.concatenate([-values_in[..., head_half:], values_in[..., :head_half]], axis=-1)
    return values_in * cosine + turned * sine


def ffn_piece(gate, upward):
    return jax.nn.gelu(gate, approximate=True) * upward


def matmul_fast(left, right):
    return jnp.dot(left, right, preferred_element_type=F32)


def left_transposed(left, right):
    return jnp.einsum("ta,tb->ab", left, right, preferred_element_type=F32)


def right_transposed(left, right):
    return jnp.einsum("ta,ba->tb", left, right, preferred_element_type=F32)


def dot(left, right, left_dim, right_dim):
    return lax.dot_general(
        left, right, (((left_dim,), (right_dim,)), ((), ())), preferred_element_type=F32
    )


def inverse_rms(values_in):
    return lax.rsqrt(jnp.mean(values_in * values_in, axis=-1, keepdims=True) + NORM_EPS)


def norm_back(values_in, gain, grad):
    inverse = inverse_rms(values_in)
    unit = values_in * inverse
    scaled = grad * gain
    grad_in = inverse * (scaled - unit * jnp.mean(scaled * unit, axis=-1, keepdims=True))
    return grad_in, jnp.sum(grad * unit, axis=0, keepdims=True)


def rotate_back(grad, cosine, sine):
    half = grad.shape[-1] // 2
    turned = grad * sine
    return grad * cosine + jnp.concatenate([turned[:, half:], -turned[:, :half]], axis=-1)


def head(h):
    return slice(h * HD, (h + 1) * HD)


def on_chip(kernel, out_shape, *operands, outside=None, scratch=()):
    vmem = pl.BlockSpec(memory_space=pltpu.VMEM)
    kept = pl.BlockSpec(memory_space=pl.ANY)
    return pl.pallas_call(
        kernel,
        out_shape=out_shape,
        in_specs=[kept if i == outside else vmem for i in range(len(operands))],
        scratch_shapes=scratch,
        out_specs=jax.tree.map(lambda _: vmem, out_shape),
        name=kernel.__name__,
    )(*operands)


def shaped(rows, columns, dtype):
    return jax.ShapeDtypeStruct((rows, columns), dtype)


def project_kernel(
    tok, w_outside, hot, hot_q, cosine, sine, slots, query, kv, lin, gains, gains_h, w, w_gains, sems
):
    n_qkv = QW + 2 * HD
    fetch_gains = pltpu.make_async_copy(
        w_outside.at[:, n_qkv : n_qkv + 128], w_gains, sems.at[0]
    )
    fetch = pltpu.make_async_copy(w_outside.at[:, :n_qkv], w, sems.at[1])
    fetch_gains.start()
    fetch.start()
    fetch_gains.wait()
    gain_rows = w_gains[...]
    all_gains = dot(gain_rows, hot[...], 0, 1)
    all_gains_h = dot(gain_rows, hot_q[...], 0, 1)
    gains[...] = all_gains[:8]
    gains_h[...] = all_gains_h[:8]
    layer_in = tok[...].astype(F32)
    normed = (layer_in * inverse_rms(layer_in) * all_gains[0:1]).astype(BF16)
    normed_slots = dot(normed, hot[...], 1, 0).astype(BF16)
    slots[...] = normed_slots
    fetch.wait()
    qkv = dot(normed_slots, w[...], 1, 0)
    lin[...] = qkv[:, : QW + HD]
    rows = tok.shape[0]

    def turned(values_in, gain):
        return rotate(values_in * inverse_rms(values_in) * gain, cosine[...], sine[...])

    for h in range(HEADS):
        query[h * rows : (h + 1) * rows, :] = turned(qkv[:, head(h)], all_gains_h[4:5]).astype(BF16)
    kv[:, :HD] = turned(qkv[:, head(HEADS)], all_gains_h[5:6]).astype(BF16)
    kv[:, HD:] = qkv[:, head(HEADS + 1)].astype(BF16)


def attend_kernel(
    query, kv, allowed, hot_o, w_outside, tok, gains, hot_f,
    probs, out_slots, branch, hidden_one, ffn_slots, w, sem,
):
    fetch = pltpu.make_async_copy(w_outside.at[:, QW + 2 * HD + 128 :], w, sem)
    fetch.start()
    rows = tok.shape[0]
    mask = allowed[...] > 0
    total = jnp.zeros(out_slots.shape, F32)
    for h in range(HEADS):
        part = slice(h * rows, (h + 1) * rows)
        raw = dot(query[part, :], kv[:, :HD], 1, 1) * HD ** (-0.5)
        scores = jnp.where(mask, raw, MASKED_SCORE)
        expo = jnp.exp(scores - jnp.max(scores, axis=-1, keepdims=True))
        prob = expo / jnp.sum(expo, axis=-1, keepdims=True)
        probs[part, :] = prob
        attended = dot(prob.astype(BF16), kv[:, HD:], 1, 0).astype(BF16)
        total += dot(attended, hot_o[head(h), :], 1, 0)
    total = total.astype(BF16)
    out_slots[...] = total
    fetch.wait()
    y = dot(total, w[...], 1, 0)
    branch[...] = y
    one = tok[...].astype(F32) + y * inverse_rms(y) * gains[1:2, :]
    hidden_one[...] = one
    ffn_in = (one * inverse_rms(one) * gains[2:3, :]).astype(BF16)
    ffn_slots[...] = dot(ffn_in, hot_f[...], 1, 0).astype(BF16)


def attend_back_kernel(
    grad_slots, hot_f, hidden_one, branch, cotangent, gains, gains_h, w_outside, hot_o,
    query, kv, probs, lin, cosine, sine,
    grad_one, grad_gains, grad_query_gain, grad_branch, kv_part, grad_lin, w, sem,
):
    fetch = pltpu.make_async_copy(w_outside.at[:, QW + 2 * HD + 128 :], w, sem)
    fetch.start()
    rows = cotangent.shape[0]
    grad_in = dot(grad_slots[...].astype(BF16), hot_f[...], 1, 1)
    part, gain_pre = norm_back(hidden_one[...], gains[2:3, :], grad_in)
    one = cotangent[...].astype(F32) + part
    grad_one[...] = one
    grad_y, gain_post = norm_back(branch[...], gains[1:2, :], one)
    grad_gains[...] = jnp.concatenate(
        [gain_post, gain_pre, jnp.zeros((6, gain_pre.shape[1]), F32)], axis=0
    )
    grad_y = grad_y.astype(BF16)
    grad_branch[...] = grad_y
    fetch.wait()
    grad_slots_o = dot(grad_y, w[...], 1, 1).astype(BF16)
    keys, values = kv[:, :HD], kv[:, HD:]
    grad_keys = jnp.zeros(keys.shape, F32)
    grad_values = jnp.zeros(values.shape, F32)
    gain_sum = jnp.zeros((1, HD), F32)
    for h in range(HEADS):
        span = slice(h * rows, (h + 1) * rows)
        grad_o = dot(grad_slots_o, hot_o[head(h), :], 1, 1).astype(BF16)
        prob = probs[span, :]
        grad_prob = dot(grad_o, values, 1, 1)
        delta = jnp.sum(grad_prob * prob, axis=-1, keepdims=True)
        grad_score = (prob * (grad_prob - delta)).astype(BF16)
        grad_keys += dot(grad_score, query[span, :], 0, 0)
        grad_values += dot(prob.astype(BF16), grad_o, 0, 0)
        grad_query = rotate_back(
            dot(grad_score, keys, 1, 0) * HD ** (-0.5), cosine[...], sine[...]
        )
        grad_head, gain = norm_back(lin[:, head(h)], gains_h[4:5, :], grad_query)
        gain_sum += gain
        grad_lin[:, head(h)] = grad_head.astype(BF16)
    kv_part[:, :HD] = grad_keys * HD ** (-0.5)
    kv_part[:, HD:] = grad_values
    grad_query_gain[...] = jnp.concatenate([gain_sum, jnp.zeros((7, HD), F32)], axis=0)


def project_back_kernel(
    grad_kv, lin, gains_h, cosine, sine, grad_query_lin, slots, hot, hot_q, grad_gains,
    grad_ffn_post, grad_query_gain, grad_lin, mine, sent,
):
    half = mine.shape[0]
    n_qkv = QW + 2 * HD
    grad_key, gain_key = norm_back(
        lin[...], gains_h[5:6, :], rotate_back(grad_kv[:, :HD], cosine[...], sine[...])
    )
    grad_lin[:, :QW] = grad_query_lin[...]
    grad_lin[:, head(HEADS)] = grad_key.astype(BF16)
    grad_lin[:, head(HEADS + 1)] = grad_kv[:, HD:].astype(BF16)
    grad_w = dot(slots[...], grad_lin[...], 0, 0)
    mine[:, :n_qkv] = grad_w[:half]
    sent[:, :n_qkv] = grad_w[half:].astype(BF16)
    wide = jnp.concatenate(
        [grad_gains[0:2, :], grad_ffn_post[...], jnp.zeros((125, hot.shape[0]), F32)], axis=0
    )
    narrow = jnp.concatenate(
        [jnp.zeros((3, HD), F32), grad_query_gain[0:1, :], gain_key, jnp.zeros((123, HD), F32)], axis=0
    )
    columns = dot(hot[...], wide.astype(BF16), 0, 1) + dot(hot_q[...], narrow.astype(BF16), 0, 1)
    mine[:, n_qkv:] = columns[:half]
    sent[:, n_qkv:] = columns[half:].astype(BF16)


def device_columns(k, c, t, n_y, units):
    start = (((t // n_y) * 4 + (k // 2) * 2 + c) * 2 * n_y + (t % n_y) * 2 + k % 2) * units
    return slice(start, start + units)


def split_columns(w_gate, w_up, core, n_t, n_y, units):
    rows = w_gate.shape[0]

    def kernel(core_ref, gate_ref, up_ref, out_ref):
        own = core_ref[0]
        for i, ref in enumerate((gate_ref, up_ref)):
            for c in range(2):
                for k in range(4):
                    for t in range(n_t):
                        out_ref[own ^ c, k, i, :, t * units : (t + 1) * units] = ref[
                            :, device_columns(k, c, t, n_y, units)
                        ]

    vmem = pl.BlockSpec(memory_space=pltpu.VMEM)
    return pl.pallas_call(
        kernel,
        out_shape=jax.ShapeDtypeStruct((2, 4, 2, rows, n_t * units), BF16),
        in_specs=[pl.BlockSpec(memory_space=pltpu.SMEM), vmem, vmem],
        out_specs=vmem,
        name="split_columns",
    )(jnp.reshape(core, (1,)), w_gate, w_up)


def join_columns(mine, other, zx, core, n_t, n_y, units):
    rows = mine.shape[2]

    def kernel(place_ref, mine_ref, other_ref, *outs):
        for i, out_ref in enumerate(outs):
            for k in range(4):
                own_core = mine_ref[place_ref[0] ^ k, i].astype(F32)
                other_core = other_ref[place_ref[0] ^ k, i].astype(F32)
                for c in range(2):
                    found = jnp.where(place_ref[1] == c, own_core, other_core)
                    for t in range(n_t):
                        out_ref[:, device_columns(k, c, t, n_y, units)] = found[
                            :, t * units : (t + 1) * units
                        ]

    vmem = pl.BlockSpec(memory_space=pltpu.VMEM)
    out = jax.ShapeDtypeStruct((rows, 8 * n_t * units), F32)
    return pl.pallas_call(
        kernel,
        out_shape=(out, out),
        in_specs=[pl.BlockSpec(memory_space=pltpu.SMEM), vmem, vmem],
        out_specs=(vmem, vmem),
        name="join_columns",
    )(jnp.stack([zx, core]), mine, other)


def body(
    tokens,
    lengths,
    w_query,
    w_key,
    w_value,
    w_out,
    w_gate,
    w_up,
    w_down,
    gain_in,
    gain_attn_post,
    gain_ffn_pre,
    gain_ffn_post,
    gain_query,
    gain_key,
    cotangent,
):
    n_ctx = lax.axis_size("ctx")
    n_dp = lax.axis_size("dp")
    n_y = n_ctx // 2
    n_zh = n_dp // 4
    n_t = n_y * n_zh
    n_dev = n_dp * n_ctx
    tok_dev, width = tokens.shape
    dp = lax.axis_index("dp")
    ctx = lax.axis_index("ctx")
    zh, zl, core = dp // 4, (dp // 2) % 2, dp % 2
    y, x = ctx // 2, ctx % 2
    zx = zl * 2 + x

    def move(values_in, dzh=0, dzl=0, dcore=0, dy=0, dx=0):
        pairs = [
            (d * n_ctx + c, (d ^ (4 * dzh + 2 * dzl + dcore)) * n_ctx + (c ^ (2 * dy + dx)))
            for d in range(n_dp)
            for c in range(n_ctx)
        ]
        return lax.ppermute(values_in, ("dp", "ctx"), pairs)

    def near(values_in, k):
        return move(values_in, dzl=k // 2, dx=k % 2)

    def pick(values_in, index, axis=0):
        return lax.dynamic_index_in_dim(values_in, index, axis, keepdims=False)

    def put(buffer, values_in, index, axis=0):
        return lax.dynamic_update_index_in_dim(buffer, values_in, index, axis)

    def after(values_in, *others):
        return lax.optimization_barrier((values_in,) + others)[0]

    def gather_zh(rows):
        return after(
            jnp.concatenate([rows] + [move(rows, dzh=j) for j in range(1, n_zh)], axis=0)
        )

    def gather_y(rows):
        return after(jnp.concatenate([rows] + [move(rows, dy=j) for j in range(1, n_y)], axis=0))

    def gather_near(rows):
        return [rows] + [near(rows, k) for k in range(1, 4)]

    def join_cores(own):
        return jnp.concatenate(own + [move(p, dcore=1) for p in own], axis=0)

    def low_sum(total, got):
        return total + got.astype(F32)

    def scatter_blocks(values_in, n, send):
        rows = values_in.shape[0] // n
        total = values_in[:rows]
        for j in range(1, n):
            total = low_sum(total, send(values_in[j * rows : (j + 1) * rows].astype(BF16), j))
        return total

    def scatter_halves(values_in):
        rows = values_in.shape[0] // 4
        low = values_in.astype(BF16)
        sent = jnp.concatenate([low[rows : 2 * rows], low[3 * rows :]], axis=0)
        came = move(sent, dx=1)
        total = low_sum(values_in[:rows], came[:rows])
        passed = low_sum(values_in[2 * rows : 3 * rows], came[rows:])
        return low_sum(total, move(passed.astype(BF16), dzl=1))

    def scatter_y(values_in):
        return scatter_blocks(values_in, n_y, lambda v, j: move(v, dy=j))

    def scatter_zh(values_in):
        return scatter_blocks(values_in, n_zh, lambda v, j: move(v, dzh=j))

    def scatter_t(values_in):
        return scatter_zh(scatter_y(values_in))

    def gather_group(values_in):
        return join_cores(gather_near(values_in))

    rows_w = w_query.shape[0]
    rows_o = w_out.shape[0]
    rows_q = gain_query.shape[0]

    def column(gain):
        return jnp.pad(gain, (0, rows_w - gain.shape[0]))[:, None]

    gain_cols = jnp.concatenate(
        [
            column(g)
            for g in (gain_in, gain_attn_post, gain_ffn_pre, gain_ffn_post, gain_query, gain_key)
        ],
        axis=1,
    )
    w_rows = jnp.concatenate([w_query, w_key, w_value], axis=1)
    n_qkv = w_rows.shape[1]
    n_wide = n_qkv + 128
    payload = jnp.concatenate(
        [
            w_rows,
            jnp.pad(gain_cols, ((0, 0), (0, 128 - 6))),
            jnp.pad(w_out, ((0, rows_w - rows_o), (0, 0))),
        ],
        axis=1,
    )
    payload_zh = gather_zh(payload)
    payload_t = gather_y(payload_zh)

    slots = after(jnp.arange(n_dev, dtype=jnp.int32), payload_zh)

    def device_of(part_core, part_zx, part_t):
        part_zh, part_y = part_t % n_zh, part_t // n_zh
        slot_dp = (zh ^ part_zh) * 4 + (part_zx // 2) * 2 + part_core
        return slot_dp * n_ctx + (y ^ part_y) * 2 + part_zx % 2

    dev_all = device_of(core ^ (slots // (4 * n_t)), zx ^ ((slots // n_t) % 4), slots % n_t)
    dev_ffn = device_of(slots % 2, (slots // 2) % 4, slots // 8)

    def one_hot(total, rows, slot_dev, padded):
        inner = jnp.arange(padded, dtype=jnp.int32)[None, :]
        natural = jnp.where(inner < rows, slot_dev[:, None] * rows + inner, -1)
        picks = jnp.arange(total, dtype=jnp.int32)[:, None] == natural.reshape(1, -1)
        return picks.astype(BF16)

    hot_w = one_hot(width, rows_w, dev_all, rows_w)
    hot_q = one_hot(HD, rows_q, dev_all, rows_w)
    hot_o = one_hot(QW, rows_o, dev_all, rows_w)
    half_w = width // 2
    hot_o = after(hot_o)
    hot_f = one_hot(width, rows_w, dev_ffn, rows_w)
    hot_w, hot_f, hot_q = after((hot_w, hot_f, hot_q))

    down_own_y = [move(after(w_down, payload_t), dy=j) for j in range(1, n_y)]
    near_w = [payload_t, move(payload_t, dx=1), move(payload_t, dzl=1)]
    near_w.append(move(near_w[2], dx=1))
    down_zh = [move(after(w_down, payload_zh), dzh=j) for j in range(1, n_zh)]
    near_w[1] = after(near_w[1], *down_zh)
    near_w[3] = after(near_w[3], *down_own_y)
    full_w = join_cores(near_w)

    units = w_down.shape[0]
    cols = n_t * units

    blocks = split_columns(w_gate, w_up, core, n_t, n_y, units)
    kept = blocks[0]
    got = move(blocks[1], dcore=1)
    paired = jnp.where(
        core == 0, jnp.concatenate([kept, got], axis=2), jnp.concatenate([got, kept], axis=2)
    )
    group_rows = jnp.zeros((2, 4, 2 * rows_w, cols), BF16)
    for k in range(4):
        piece = pick(paired, zx ^ k)
        group_rows = put(group_rows, near(piece, k) if k else piece, zx ^ k, 1)
    group_rows = group_rows.reshape(2, 8 * rows_w, cols)

    down_zh = [after(p, full_w) for p in down_zh]

    def join_down(held_by, down_far):
        joined = jnp.zeros((n_zh, n_y, units, width), BF16)
        for j in range(n_y):
            line = [down_own_y[j - 1]] + down_far[j - 1] if j else [w_down] + down_zh
            for i in range(n_zh):
                part = after(line[i], held_by)[None, None]
                joined = lax.dynamic_update_slice(joined, part, (zh ^ i, y ^ j, 0, 0))
        return joined.reshape(cols, width)

    gate_zh = [move(group_rows[0], dzh=j) for j in range(1, n_zh)]
    up_zh = [move(group_rows[1], dzh=j) for j in range(1, n_zh)]
    full_w = after(full_w, *gate_zh)
    full_qkv = full_w[:, :n_qkv]
    gate_far = [[move(p, dy=j) for p in gate_zh] for j in range(1, n_y)]
    wide_y = [move(group_rows, dy=j) for j in range(1, n_y)]

    def join_groups(i, came_zh, far):
        parts = [group_rows[i]] + came_zh
        for own, forwarded in zip(wide_y, far):
            parts = parts + [own[i]] + forwarded
        return jnp.concatenate(parts, axis=0)

    seq_lengths = lengths[0]
    inner = jnp.arange(tok_dev, dtype=jnp.int32)
    local_places = places_of(jnp.full_like(inner, ctx), inner, tok_dev, n_ctx)
    row_owner = ctx ^ jnp.arange(n_ctx, dtype=jnp.int32)
    row_places = places_of(row_owner[:, None], inner[None, :], tok_dev, n_ctx).reshape(-1)
    local_segment, local_relative = segment_info(local_places, seq_lengths)
    row_segment, row_relative = segment_info(row_places, seq_lengths)
    cosine, sine = rope_tables(local_relative)

    def swap_c(values_in, j):
        return move(values_in, dy=j // 2, dx=j % 2)

    layer_in = tokens.astype(F32)
    row_len = n_ctx * tok_dev
    normed_slots, query_low, own_kv, qk_lin, gains, gains_h = on_chip(
        project_kernel,
        (
            shaped(tok_dev, width, BF16),
            shaped(HEADS * tok_dev, HD, BF16),
            shaped(tok_dev, 2 * HD, BF16),
            shaped(tok_dev, QW + HD, F32),
            shaped(8, width, F32),
            shaped(8, HD, F32),
        ),
        tokens, after(full_w, *wide_y), hot_w, hot_q, cosine, sine,
        outside=1,
        scratch=[
            pltpu.VMEM((width, n_qkv), BF16),
            pltpu.VMEM((width, 128), BF16),
            pltpu.SemaphoreType.DMA((2,)),
        ],
    )
    out_scratch = [pltpu.VMEM((width, width), BF16), pltpu.SemaphoreType.DMA]
    row_kv = jnp.concatenate([own_kv] + [swap_c(own_kv, j) for j in range(1, n_ctx)], axis=0)
    up_zh = [after(p, row_kv) for p in up_zh]
    down_far = [[move(after(p, row_kv), dy=j) for p in down_zh] for j in range(1, n_y)]
    allowed = (local_segment[:, None] == row_segment[None, :]) & (
        row_places[None, :] <= local_places[:, None]
    )
    up_far = [[move(p, dy=j) for p in up_zh] for j in range(1, n_y)]
    probs, out_slots, branch_attn, hidden_one, ffn_slots = on_chip(
        attend_kernel,
        (
            shaped(HEADS * tok_dev, row_len, F32),
            shaped(tok_dev, width, BF16),
            shaped(tok_dev, width, F32),
            shaped(tok_dev, width, F32),
            shaped(tok_dev, width, BF16),
        ),
        after(query_low, *up_zh), after(row_kv, *sum(gate_far, [])), allowed.astype(F32), hot_o, full_w,
        tokens, gains, hot_f, outside=4, scratch=out_scratch,
    )

    half = 4 * tok_dev

    def scatter_group(left, right):
        far = right(left[half:]).astype(BF16)
        total = low_sum(right(left[:half]), move(far, dcore=1))
        return scatter_blocks(total, 4, near)

    ffn_source = gather_group(ffn_slots)
    full_gate = join_groups(0, gate_zh, gate_far)
    full_up = join_groups(1, up_zh, up_far)
    gate = matmul_fast(ffn_source, full_gate)
    upward = matmul_fast(ffn_source, full_up)
    full_down = after(join_down(gate, down_far))
    hidden, pull_ffn = jax.vjp(ffn_piece, gate, upward)
    hidden_low = hidden.astype(BF16)
    branch_ffn = scatter_group(hidden_low, lambda v: matmul_fast(v, full_down))
    post_ffn, pull_ffn_post = jax.vjp(rms_norm, branch_ffn, gains[3])
    layer_out = (hidden_one + post_ffn).astype(BF16)

    grad_out = cotangent.astype(F32)
    grad_branch_ffn, grad_ffn_post = pull_ffn_post(grad_out)
    grad_branch_rows = gather_group(grad_branch_ffn.astype(BF16))
    grad_hidden = right_transposed(grad_branch_rows, full_down)
    grad_gate, grad_upward = pull_ffn(grad_hidden)
    grad_gate_low = grad_gate.astype(BF16)
    grad_up_low = grad_upward.astype(BF16)

    def grad_terms(part):
        return right_transposed(grad_gate_low[part], full_gate) + right_transposed(
            grad_up_low[part], full_up
        )

    grad_far = move(grad_terms(slice(half, None)).astype(BF16), dcore=1)
    grad_chip = low_sum(grad_terms(slice(None, half)), grad_far)
    grad_came = [
        near(grad_chip[j * tok_dev : (j + 1) * tok_dev].astype(BF16), j) for j in range(1, 4)
    ]
    grad_ffn_slots = grad_chip[:tok_dev]
    for came in grad_came:
        grad_ffn_slots = low_sum(grad_ffn_slots, came)
    held = after(ffn_source, grad_chip)
    rows_first = Layout(major_to_minor=(0, 1))
    grad_w_gate = with_layout_constraint(left_transposed(held, grad_gate_low), rows_first)
    grad_w_up = with_layout_constraint(left_transposed(after(held, grad_came[0]), grad_up_low), rows_first)
    grad_down = left_transposed(after(hidden_low, grad_came[0]), grad_branch_rows)
    grad_down = grad_down.reshape(n_zh, n_y, units, width)

    grad_hidden_one, grad_gains, grad_query_gain, grad_attn_low, kv_part, grad_query_lin = on_chip(
        attend_back_kernel,
        (
            shaped(tok_dev, width, F32),
            shaped(8, width, F32),
            shaped(8, HD, F32),
            shaped(tok_dev, width, BF16),
            shaped(row_len, 2 * HD, F32),
            shaped(tok_dev, QW, BF16),
        ),
        after(grad_ffn_slots, grad_w_up, grad_down), hot_f, hidden_one, branch_attn, cotangent, gains, gains_h, full_w,
        hot_o, query_low, row_kv, probs, qk_lin, cosine, sine, outside=7, scratch=out_scratch,
    )
    out_chip = scatter_blocks(
        left_transposed(out_slots, grad_attn_low), 2, lambda v, j: move(v, dcore=j)
    )
    out_near = scatter_halves(out_chip)
    rows_y = width // n_y
    gate_came = [
        after(move(grad_w_gate[j * rows_y : (j + 1) * rows_y].astype(BF16), dy=j), grad_query_lin)
        for j in range(1, n_y)
    ]
    grad_kv = scatter_blocks(after(kv_part, *gate_came), n_ctx, swap_c)
    gate_y = grad_w_gate[:rows_y]
    for came in gate_came:
        gate_y = low_sum(gate_y, came)
    grad_qkv_low, chip_mine, chip_sent = on_chip(
        project_back_kernel,
        (
            shaped(tok_dev, n_qkv, BF16),
            shaped(half_w, n_wide, F32),
            shaped(half_w, n_wide, BF16),
        ),
        after(grad_kv, gate_y, out_chip), after(qk_lin, kv_part)[:, QW:], gains_h, cosine, sine, grad_query_lin, normed_slots,
        hot_w, hot_q, grad_gains, grad_ffn_post[None, :], grad_query_gain,
    )
    up_y = scatter_blocks(
        grad_w_up, n_y, lambda v, j: after(move(after(v, grad_kv), dy=j), grad_qkv_low)
    )
    chip_w = low_sum(chip_mine, move(chip_sent, dcore=1))
    rows_n = chip_w.shape[0] // 4
    chip_low = after(chip_w, up_y).astype(BF16)
    chip_sent_x = jnp.concatenate([chip_low[rows_n : 2 * rows_n], chip_low[3 * rows_n :]], axis=0)
    chip_came = move(chip_sent_x, dx=1)
    chip_passed = low_sum(chip_w[2 * rows_n : 3 * rows_n], chip_came[rows_n:]).astype(BF16)
    down_y = pick(grad_down, y, 1)
    for j in range(1, n_y):
        sent = after(pick(grad_down, y ^ j, 1).astype(BF16), up_y)
        down_y = low_sum(down_y, after(move(sent, dy=j), chip_passed))
    near_w = low_sum(
        low_sum(chip_w[:rows_n], chip_came[:rows_n]), move(after(chip_passed, down_y), dzl=1)
    )
    mine_w = scatter_t(jnp.concatenate([near_w, out_near], axis=1))
    out_w_out = mine_w[:rows_o, n_wide:]
    sums = [
        scatter_blocks(gate_y, n_zh, lambda v, j: after(move(v, dzh=j), near_w)),
        scatter_blocks(up_y, n_zh, lambda v, j: after(move(v, dzh=j), near_w)),
    ]
    sums = jnp.stack([v.astype(BF16).reshape(4, 2, rows_w, cols) for v in sums], axis=1)
    owned = jnp.stack([near(pick(sums, zx ^ k), k) if k else pick(sums, zx) for k in range(4)])
    mine = pick(owned, core, 2)
    other = move(pick(owned, 1 - core, 2), dcore=1)
    out_gate, out_up = join_columns(mine, other, zx, core, n_t, n_y, units)
    out_down = pick(down_y, zh)
    for j in range(1, n_zh):
        out_down = low_sum(out_down, move(pick(down_y, zh ^ j).astype(BF16), dzh=j))
    grad_normed = right_transposed(
        right_transposed(after(grad_qkv_low, chip_w), full_qkv).astype(BF16), hot_w
    )
    grad_in_part, _ = norm_back(layer_in, gains[0], grad_normed)
    input_grad = (grad_hidden_one + grad_in_part).astype(BF16)
    out_gain_in = jnp.sum(w_rows.astype(F32) * mine_w[:, :n_qkv], axis=1) / gain_in.astype(F32)
    gain_out = mine_w[:, n_qkv:n_wide]
    return (
        layer_out,
        input_grad,
        mine_w[:, :QW],
        mine_w[:, QW : QW + HD],
        mine_w[:, QW + HD : n_qkv],
        out_w_out,
        out_gate,
        out_up,
        out_down,
        out_gain_in,
        gain_out[:, 0],
        gain_out[:, 1],
        gain_out[:, 2],
        gain_out[:rows_q, 3],
        gain_out[:rows_q, 4],
    )


def solution(mesh):
    split = P(("dp", "ctx"), None)
    split_1d = P(("dp", "ctx"))
    in_specs = (split, P("dp", None)) + (split,) * 7 + (split_1d,) * 6 + (split,)
    out_specs = (split,) * 9 + (split_1d,) * 6
    return jax.shard_map(body, mesh=mesh, in_specs=in_specs, out_specs=out_specs, check_vma=False)
```

```python
import jax
import jax.numpy as jnp
from jax import lax
from jax.experimental import pallas as pl
from jax.experimental.layout import Layout, with_layout_constraint
from jax.experimental.pallas import tpu as pltpu
from jax.sharding import PartitionSpec as P

HEADS = 4
HD = 256
QW = HEADS * HD


NORM_EPS = 1e-06
ROPE_BASE = 1000000.0
MASKED_SCORE = -1e30
F32 = jnp.float32
BF16 = jnp.bfloat16


def rms_norm(values_in, gain):
    return (
        values_in
        * lax.rsqrt(jnp.mean(values_in * values_in, axis=-1, keepdims=True) + NORM_EPS)
        * gain
    )


def places_of(owner, inner, tok_dev, n_ctx):
    half_len = tok_dev // 2
    block_id = jnp.where(inner < half_len, owner, 2 * n_ctx - 1 - owner)
    return block_id * half_len + inner % half_len


def segment_info(places, seq_lengths):
    ends = jnp.cumsum(seq_lengths)
    passed = places[:, None] >= ends[None, :]
    segment = jnp.sum(passed.astype(jnp.int32), axis=-1)
    start = jnp.sum(jnp.where(passed, seq_lengths[None, :], 0), axis=-1)
    return (segment, places - start)


def rope_tables(relative):
    head_half = HD // 2
    freqs = ROPE_BASE ** (-(jnp.arange(head_half, dtype=F32) * 2.0 / HD))
    angles = relative.astype(F32)[:, None] * freqs[None, :]
    cosine = jnp.concatenate([jnp.cos(angles), jnp.cos(angles)], axis=-1)
    sine = jnp.concatenate([jnp.sin(angles), jnp.sin(angles)], axis=-1)
    return (cosine, sine)


def rotate(values_in, cosine, sine):
    head_half = values_in.shape[-1] // 2
    turned = jnp.concatenate([-values_in[..., head_half:], values_in[..., :head_half]], axis=-1)
    return values_in * cosine + turned * sine


def ffn_piece(gate, upward):
    return jax.nn.gelu(gate, approximate=True) * upward


def matmul_fast(left, right):
    return jnp.dot(left, right, preferred_element_type=F32)


def left_transposed(left, right):
    return jnp.einsum("ta,tb->ab", left, right, preferred_element_type=F32)


def right_transposed(left, right):
    return jnp.einsum("ta,ba->tb", left, right, preferred_element_type=F32)


def dot(left, right, left_dim, right_dim):
    return lax.dot_general(
        left, right, (((left_dim,), (right_dim,)), ((), ())), preferred_element_type=F32
    )


def inverse_rms(values_in):
    return lax.rsqrt(jnp.mean(values_in * values_in, axis=-1, keepdims=True) + NORM_EPS)


def norm_back(values_in, gain, grad):
    inverse = inverse_rms(values_in)
    unit = values_in * inverse
    scaled = grad * gain
    grad_in = inverse * (scaled - unit * jnp.mean(scaled * unit, axis=-1, keepdims=True))
    return grad_in, jnp.sum(grad * unit, axis=0, keepdims=True)


def rotate_back(grad, cosine, sine):
    half = grad.shape[-1] // 2
    turned = grad * sine
    return grad * cosine + jnp.concatenate([turned[:, half:], -turned[:, :half]], axis=-1)


def head(h):
    return slice(h * HD, (h + 1) * HD)


def on_chip(kernel, out_shape, *operands, outside=None, scratch=()):
    vmem = pl.BlockSpec(memory_space=pltpu.VMEM)
    kept = pl.BlockSpec(memory_space=pl.ANY)
    return pl.pallas_call(
        kernel,
        out_shape=out_shape,
        in_specs=[kept if i == outside else vmem for i in range(len(operands))],
        scratch_shapes=scratch,
        out_specs=jax.tree.map(lambda _: vmem, out_shape),
        name=kernel.__name__,
    )(*operands)


def shaped(rows, columns, dtype):
    return jax.ShapeDtypeStruct((rows, columns), dtype)


def project_kernel(
    tok, w_outside, hot, hot_q, cosine, sine, slots, query, kv, lin, gains, gains_h, w, w_gains, sems
):
    n_qkv = QW + 2 * HD
    fetch_gains = pltpu.make_async_copy(
        w_outside.at[:, n_qkv : n_qkv + 128], w_gains, sems.at[0]
    )
    fetch = pltpu.make_async_copy(w_outside.at[:, :n_qkv], w, sems.at[1])
    fetch_gains.start()
    fetch.start()
    fetch_gains.wait()
    gain_rows = w_gains[...]
    all_gains = dot(gain_rows, hot[...], 0, 1)
    all_gains_h = dot(gain_rows, hot_q[...], 0, 1)
    gains[...] = all_gains[:8]
    gains_h[...] = all_gains_h[:8]
    layer_in = tok[...].astype(F32)
    normed = (layer_in * inverse_rms(layer_in) * all_gains[0:1]).astype(BF16)
    normed_slots = dot(normed, hot[...], 1, 0).astype(BF16)
    slots[...] = normed_slots
    fetch.wait()
    qkv = dot(normed_slots, w[...], 1, 0)
    lin[...] = qkv[:, : QW + HD]
    rows = tok.shape[0]

    def turned(values_in, gain):
        return rotate(values_in * inverse_rms(values_in) * gain, cosine[...], sine[...])

    for h in range(HEADS):
        query[h * rows : (h + 1) * rows, :] = turned(qkv[:, head(h)], all_gains_h[4:5]).astype(BF16)
    kv[:, :HD] = turned(qkv[:, head(HEADS)], all_gains_h[5:6]).astype(BF16)
    kv[:, HD:] = qkv[:, head(HEADS + 1)].astype(BF16)


def attend_kernel(
    query, kv, allowed, hot_o, w_outside, tok, gains, hot_f,
    probs, out_slots, branch, hidden_one, ffn_slots, w, sem,
):
    fetch = pltpu.make_async_copy(w_outside.at[:, QW + 2 * HD + 128 :], w, sem)
    fetch.start()
    rows = tok.shape[0]
    mask = allowed[...] > 0
    total = jnp.zeros(out_slots.shape, F32)
    for h in range(HEADS):
        part = slice(h * rows, (h + 1) * rows)
        raw = dot(query[part, :], kv[:, :HD], 1, 1) * HD ** (-0.5)
        scores = jnp.where(mask, raw, MASKED_SCORE)
        expo = jnp.exp(scores - jnp.max(scores, axis=-1, keepdims=True))
        prob = expo / jnp.sum(expo, axis=-1, keepdims=True)
        probs[part, :] = prob
        attended = dot(prob.astype(BF16), kv[:, HD:], 1, 0).astype(BF16)
        total += dot(attended, hot_o[head(h), :], 1, 0)
    total = total.astype(BF16)
    out_slots[...] = total
    fetch.wait()
    y = dot(total, w[...], 1, 0)
    branch[...] = y
    one = tok[...].astype(F32) + y * inverse_rms(y) * gains[1:2, :]
    hidden_one[...] = one
    ffn_in = (one * inverse_rms(one) * gains[2:3, :]).astype(BF16)
    ffn_slots[...] = dot(ffn_in, hot_f[...], 1, 0).astype(BF16)


def attend_back_kernel(
    grad_slots, hot_f, hidden_one, branch, cotangent, gains, gains_h, w_outside, hot_o,
    query, kv, probs, lin, cosine, sine,
    grad_one, grad_gains, grad_query_gain, grad_branch, kv_part, grad_lin, w, sem,
):
    fetch = pltpu.make_async_copy(w_outside.at[:, QW + 2 * HD + 128 :], w, sem)
    fetch.start()
    rows = cotangent.shape[0]
    grad_in = dot(grad_slots[...].astype(BF16), hot_f[...], 1, 1)
    part, gain_pre = norm_back(hidden_one[...], gains[2:3, :], grad_in)
    one = cotangent[...].astype(F32) + part
    grad_one[...] = one
    grad_y, gain_post = norm_back(branch[...], gains[1:2, :], one)
    grad_gains[...] = jnp.concatenate(
        [gain_post, gain_pre, jnp.zeros((6, gain_pre.shape[1]), F32)], axis=0
    )
    grad_y = grad_y.astype(BF16)
    grad_branch[...] = grad_y
    fetch.wait()
    grad_slots_o = dot(grad_y, w[...], 1, 1).astype(BF16)
    keys, values = kv[:, :HD], kv[:, HD:]
    grad_keys = jnp.zeros(keys.shape, F32)
    grad_values = jnp.zeros(values.shape, F32)
    gain_sum = jnp.zeros((1, HD), F32)
    for h in range(HEADS):
        span = slice(h * rows, (h + 1) * rows)
        grad_o = dot(grad_slots_o, hot_o[head(h), :], 1, 1).astype(BF16)
        prob = probs[span, :]
        grad_prob = dot(grad_o, values, 1, 1)
        delta = jnp.sum(grad_prob * prob, axis=-1, keepdims=True)
        grad_score = (prob * (grad_prob - delta)).astype(BF16)
        grad_keys += dot(grad_score, query[span, :], 0, 0)
        grad_values += dot(prob.astype(BF16), grad_o, 0, 0)
        grad_query = rotate_back(
            dot(grad_score, keys, 1, 0) * HD ** (-0.5), cosine[...], sine[...]
        )
        grad_head, gain = norm_back(lin[:, head(h)], gains_h[4:5, :], grad_query)
        gain_sum += gain
        grad_lin[:, head(h)] = grad_head.astype(BF16)
    kv_part[:, :HD] = grad_keys * HD ** (-0.5)
    kv_part[:, HD:] = grad_values
    grad_query_gain[...] = jnp.concatenate([gain_sum, jnp.zeros((7, HD), F32)], axis=0)


def project_back_kernel(
    grad_kv, lin, gains_h, cosine, sine, grad_query_lin, slots, hot, hot_q, grad_gains,
    grad_ffn_post, grad_query_gain, grad_lin, mine, sent,
):
    half = mine.shape[0]
    n_qkv = QW + 2 * HD
    grad_key, gain_key = norm_back(
        lin[:, QW:], gains_h[5:6, :], rotate_back(grad_kv[:, :HD], cosine[...], sine[...])
    )
    grad_lin[:, :QW] = grad_query_lin[...]
    grad_lin[:, head(HEADS)] = grad_key.astype(BF16)
    grad_lin[:, head(HEADS + 1)] = grad_kv[:, HD:].astype(BF16)
    grad_w = dot(slots[...], grad_lin[...], 0, 0)
    mine[:, :n_qkv] = grad_w[:half]
    sent[:, :n_qkv] = grad_w[half:].astype(BF16)
    wide = jnp.concatenate(
        [grad_gains[0:2, :], grad_ffn_post[...], jnp.zeros((125, hot.shape[0]), F32)], axis=0
    )
    narrow = jnp.concatenate(
        [jnp.zeros((3, HD), F32), grad_query_gain[0:1, :], gain_key, jnp.zeros((123, HD), F32)], axis=0
    )
    columns = dot(hot[...], wide.astype(BF16), 0, 1) + dot(hot_q[...], narrow.astype(BF16), 0, 1)
    mine[:, n_qkv:] = columns[:half]
    sent[:, n_qkv:] = columns[half:].astype(BF16)


def device_columns(k, c, t, n_y, units):
    start = (((t // n_y) * 4 + (k // 2) * 2 + c) * 2 * n_y + (t % n_y) * 2 + k % 2) * units
    return slice(start, start + units)


def split_columns(w_gate, w_up, core, n_t, n_y, units):
    rows = w_gate.shape[0]

    def kernel(core_ref, gate_ref, up_ref, out_ref):
        own = core_ref[0]
        for i, ref in enumerate((gate_ref, up_ref)):
            for c in range(2):
                for k in range(4):
                    for t in range(n_t):
                        out_ref[own ^ c, k, i, :, t * units : (t + 1) * units] = ref[
                            :, device_columns(k, c, t, n_y, units)
                        ]

    vmem = pl.BlockSpec(memory_space=pltpu.VMEM)
    return pl.pallas_call(
        kernel,
        out_shape=jax.ShapeDtypeStruct((2, 4, 2, rows, n_t * units), BF16),
        in_specs=[pl.BlockSpec(memory_space=pltpu.SMEM), vmem, vmem],
        out_specs=vmem,
        name="split_columns",
    )(jnp.reshape(core, (1,)), w_gate, w_up)


def join_columns(mine, other, zx, core, n_t, n_y, units):
    rows = mine.shape[2]

    def kernel(place_ref, mine_ref, other_ref, *outs):
        for i, out_ref in enumerate(outs):
            for k in range(4):
                own_core = mine_ref[place_ref[0] ^ k, i].astype(F32)
                other_core = other_ref[place_ref[0] ^ k, i].astype(F32)
                for c in range(2):
                    found = jnp.where(place_ref[1] == c, own_core, other_core)
                    for t in range(n_t):
                        out_ref[:, device_columns(k, c, t, n_y, units)] = found[
                            :, t * units : (t + 1) * units
                        ]

    vmem = pl.BlockSpec(memory_space=pltpu.VMEM)
    out = jax.ShapeDtypeStruct((rows, 8 * n_t * units), F32)
    return pl.pallas_call(
        kernel,
        out_shape=(out, out),
        in_specs=[pl.BlockSpec(memory_space=pltpu.SMEM), vmem, vmem],
        out_specs=(vmem, vmem),
        name="join_columns",
    )(jnp.stack([zx, core]), mine, other)


def body(
    tokens,
    lengths,
    w_query,
    w_key,
    w_value,
    w_out,
    w_gate,
    w_up,
    w_down,
    gain_in,
    gain_attn_post,
    gain_ffn_pre,
    gain_ffn_post,
    gain_query,
    gain_key,
    cotangent,
):
    n_ctx = lax.axis_size("ctx")
    n_dp = lax.axis_size("dp")
    n_y = n_ctx // 2
    n_zh = n_dp // 4
    n_t = n_y * n_zh
    n_dev = n_dp * n_ctx
    tok_dev, width = tokens.shape
    dp = lax.axis_index("dp")
    ctx = lax.axis_index("ctx")
    zh, zl, core = dp // 4, (dp // 2) % 2, dp % 2
    y, x = ctx // 2, ctx % 2
    zx = zl * 2 + x

    def move(values_in, dzh=0, dzl=0, dcore=0, dy=0, dx=0):
        pairs = [
            (d * n_ctx + c, (d ^ (4 * dzh + 2 * dzl + dcore)) * n_ctx + (c ^ (2 * dy + dx)))
            for d in range(n_dp)
            for c in range(n_ctx)
        ]
        return lax.ppermute(values_in, ("dp", "ctx"), pairs)

    def near(values_in, k):
        return move(values_in, dzl=k // 2, dx=k % 2)

    def pick(values_in, index, axis=0):
        return lax.dynamic_index_in_dim(values_in, index, axis, keepdims=False)

    def put(buffer, values_in, index, axis=0):
        return lax.dynamic_update_index_in_dim(buffer, values_in, index, axis)

    def after(values_in, *others):
        return lax.optimization_barrier((values_in,) + others)[0]

    def gather_zh(rows):
        return after(
            jnp.concatenate([rows] + [move(rows, dzh=j) for j in range(1, n_zh)], axis=0)
        )

    def gather_y(rows):
        return after(jnp.concatenate([rows] + [move(rows, dy=j) for j in range(1, n_y)], axis=0))

    def gather_near(rows):
        return [rows] + [near(rows, k) for k in range(1, 4)]

    def join_cores(own):
        return jnp.concatenate(own + [move(p, dcore=1) for p in own], axis=0)

    def low_sum(total, got):
        return total + got.astype(F32)

    def scatter_blocks(values_in, n, send):
        rows = values_in.shape[0] // n
        total = values_in[:rows]
        for j in range(1, n):
            total = low_sum(total, send(values_in[j * rows : (j + 1) * rows].astype(BF16), j))
        return total

    def scatter_halves(values_in):
        rows = values_in.shape[0] // 4
        low = values_in.astype(BF16)
        sent = jnp.concatenate([low[rows : 2 * rows], low[3 * rows :]], axis=0)
        came = move(sent, dx=1)
        total = low_sum(values_in[:rows], came[:rows])
        passed = low_sum(values_in[2 * rows : 3 * rows], came[rows:])
        return low_sum(total, move(passed.astype(BF16), dzl=1))

    def scatter_y(values_in):
        return scatter_blocks(values_in, n_y, lambda v, j: move(v, dy=j))

    def scatter_zh(values_in):
        return scatter_blocks(values_in, n_zh, lambda v, j: move(v, dzh=j))

    def scatter_t(values_in):
        return scatter_zh(scatter_y(values_in))

    def gather_group(values_in):
        return join_cores(gather_near(values_in))

    rows_w = w_query.shape[0]
    rows_o = w_out.shape[0]
    rows_q = gain_query.shape[0]

    def column(gain):
        return jnp.pad(gain, (0, rows_w - gain.shape[0]))[:, None]

    gain_cols = jnp.concatenate(
        [
            column(g)
            for g in (gain_in, gain_attn_post, gain_ffn_pre, gain_ffn_post, gain_query, gain_key)
        ],
        axis=1,
    )
    w_rows = jnp.concatenate([w_query, w_key, w_value], axis=1)
    n_qkv = w_rows.shape[1]
    n_wide = n_qkv + 128
    payload = jnp.concatenate(
        [
            w_rows,
            jnp.pad(gain_cols, ((0, 0), (0, 128 - 6))),
            jnp.pad(w_out, ((0, rows_w - rows_o), (0, 0))),
        ],
        axis=1,
    )
    payload_zh = gather_zh(payload)
    payload_t = gather_y(payload_zh)

    slots = after(jnp.arange(n_dev, dtype=jnp.int32), payload_zh)

    def device_of(part_core, part_zx, part_t):
        part_zh, part_y = part_t % n_zh, part_t // n_zh
        slot_dp = (zh ^ part_zh) * 4 + (part_zx // 2) * 2 + part_core
        return slot_dp * n_ctx + (y ^ part_y) * 2 + part_zx % 2

    dev_all = device_of(core ^ (slots // (4 * n_t)), zx ^ ((slots // n_t) % 4), slots % n_t)
    dev_ffn = device_of(slots % 2, (slots // 2) % 4, slots // 8)

    def one_hot(total, rows, slot_dev, padded):
        inner = jnp.arange(padded, dtype=jnp.int32)[None, :]
        natural = jnp.where(inner < rows, slot_dev[:, None] * rows + inner, -1)
        picks = jnp.arange(total, dtype=jnp.int32)[:, None] == natural.reshape(1, -1)
        return picks.astype(BF16)

    hot_w = one_hot(width, rows_w, dev_all, rows_w)
    hot_q = one_hot(HD, rows_q, dev_all, rows_w)
    hot_o = one_hot(QW, rows_o, dev_all, rows_w)
    half_w = width // 2
    hot_o = after(hot_o)
    hot_f = one_hot(width, rows_w, dev_ffn, rows_w)
    hot_w, hot_f, hot_q = after((hot_w, hot_f, hot_q))

    down_own_y = [move(after(w_down, payload_t), dy=j) for j in range(1, n_y)]
    near_w = [payload_t, move(payload_t, dx=1), move(payload_t, dzl=1)]
    near_w.append(move(near_w[2], dx=1))
    down_zh = [move(after(w_down, payload_zh), dzh=j) for j in range(1, n_zh)]
    near_w[1] = after(near_w[1], *down_zh)
    near_w[3] = after(near_w[3], *down_own_y)
    full_w = join_cores(near_w)

    units = w_down.shape[0]
    cols = n_t * units

    blocks = split_columns(w_gate, w_up, core, n_t, n_y, units)
    kept = blocks[0]
    got = move(blocks[1], dcore=1)
    paired = jnp.where(
        core == 0, jnp.concatenate([kept, got], axis=2), jnp.concatenate([got, kept], axis=2)
    )
    group_rows = jnp.zeros((2, 4, 2 * rows_w, cols), BF16)
    for k in range(4):
        piece = pick(paired, zx ^ k)
        group_rows = put(group_rows, near(piece, k) if k else piece, zx ^ k, 1)
    group_rows = group_rows.reshape(2, 8 * rows_w, cols)

    down_zh = [after(p, full_w) for p in down_zh]

    def join_down(held_by, down_far):
        joined = jnp.zeros((n_zh, n_y, units, width), BF16)
        for j in range(n_y):
            line = [down_own_y[j - 1]] + down_far[j - 1] if j else [w_down] + down_zh
            for i in range(n_zh):
                part = after(line[i], held_by)[None, None]
                joined = lax.dynamic_update_slice(joined, part, (zh ^ i, y ^ j, 0, 0))
        return joined.reshape(cols, width)

    gate_zh = [move(group_rows[0], dzh=j) for j in range(1, n_zh)]
    up_zh = [move(group_rows[1], dzh=j) for j in range(1, n_zh)]
    full_w = after(full_w, *gate_zh)
    full_qkv = full_w[:, :n_qkv]
    gate_far = [[move(p, dy=j) for p in gate_zh] for j in range(1, n_y)]
    wide_y = [move(group_rows, dy=j) for j in range(1, n_y)]

    def join_groups(i, came_zh, far):
        parts = [group_rows[i]] + came_zh
        for own, forwarded in zip(wide_y, far):
            parts = parts + [own[i]] + forwarded
        return jnp.concatenate(parts, axis=0)

    seq_lengths = lengths[0]
    inner = jnp.arange(tok_dev, dtype=jnp.int32)
    local_places = places_of(jnp.full_like(inner, ctx), inner, tok_dev, n_ctx)
    row_owner = ctx ^ jnp.arange(n_ctx, dtype=jnp.int32)
    row_places = places_of(row_owner[:, None], inner[None, :], tok_dev, n_ctx).reshape(-1)
    local_segment, local_relative = segment_info(local_places, seq_lengths)
    row_segment, row_relative = segment_info(row_places, seq_lengths)
    cosine, sine = rope_tables(local_relative)

    def swap_c(values_in, j):
        return move(values_in, dy=j // 2, dx=j % 2)

    layer_in = tokens.astype(F32)
    row_len = n_ctx * tok_dev
    normed_slots, query_low, own_kv, qk_lin, gains, gains_h = on_chip(
        project_kernel,
        (
            shaped(tok_dev, width, BF16),
            shaped(HEADS * tok_dev, HD, BF16),
            shaped(tok_dev, 2 * HD, BF16),
            shaped(tok_dev, QW + HD, F32),
            shaped(8, width, F32),
            shaped(8, HD, F32),
        ),
        tokens, after(full_w, *wide_y), hot_w, hot_q, cosine, sine,
        outside=1,
        scratch=[
            pltpu.VMEM((width, n_qkv), BF16),
            pltpu.VMEM((width, 128), BF16),
            pltpu.SemaphoreType.DMA((2,)),
        ],
    )
    out_scratch = [pltpu.VMEM((width, width), BF16), pltpu.SemaphoreType.DMA]
    row_kv = jnp.concatenate([own_kv] + [swap_c(own_kv, j) for j in range(1, n_ctx)], axis=0)
    up_zh = [after(p, row_kv) for p in up_zh]
    down_far = [[move(after(p, row_kv), dy=j) for p in down_zh] for j in range(1, n_y)]
    allowed = (local_segment[:, None] == row_segment[None, :]) & (
        row_places[None, :] <= local_places[:, None]
    )
    up_far = [[move(p, dy=j) for p in up_zh] for j in range(1, n_y)]
    probs, out_slots, branch_attn, hidden_one, ffn_slots = on_chip(
        attend_kernel,
        (
            shaped(HEADS * tok_dev, row_len, F32),
            shaped(tok_dev, width, BF16),
            shaped(tok_dev, width, F32),
            shaped(tok_dev, width, F32),
            shaped(tok_dev, width, BF16),
        ),
        after(query_low, *up_zh), after(row_kv, *sum(gate_far, [])), allowed.astype(F32), hot_o, full_w,
        tokens, gains, hot_f, outside=4, scratch=out_scratch,
    )

    half = 4 * tok_dev

    def scatter_group(left, right):
        far = right(left[half:]).astype(BF16)
        total = low_sum(right(left[:half]), move(far, dcore=1))
        return scatter_blocks(total, 4, near)

    ffn_source = gather_group(ffn_slots)
    full_gate = join_groups(0, gate_zh, gate_far)
    full_up = join_groups(1, up_zh, up_far)
    gate = matmul_fast(ffn_source, full_gate)
    upward = matmul_fast(ffn_source, full_up)
    full_down = after(join_down(gate, down_far))
    hidden, pull_ffn = jax.vjp(ffn_piece, gate, upward)
    hidden_low = hidden.astype(BF16)
    branch_ffn = scatter_group(hidden_low, lambda v: matmul_fast(v, full_down))
    post_ffn, pull_ffn_post = jax.vjp(rms_norm, branch_ffn, gains[3])
    layer_out = (hidden_one + post_ffn).astype(BF16)

    grad_out = cotangent.astype(F32)
    grad_branch_ffn, grad_ffn_post = pull_ffn_post(grad_out)
    grad_branch_rows = gather_group(grad_branch_ffn.astype(BF16))
    grad_hidden = right_transposed(grad_branch_rows, full_down)
    grad_gate, grad_upward = pull_ffn(grad_hidden)
    grad_gate_low = grad_gate.astype(BF16)
    grad_up_low = grad_upward.astype(BF16)

    def grad_terms(part):
        return right_transposed(grad_gate_low[part], full_gate) + right_transposed(
            grad_up_low[part], full_up
        )

    grad_far = move(grad_terms(slice(half, None)).astype(BF16), dcore=1)
    grad_chip = low_sum(grad_terms(slice(None, half)), grad_far)
    grad_came = [
        near(grad_chip[j * tok_dev : (j + 1) * tok_dev].astype(BF16), j) for j in range(1, 4)
    ]
    grad_ffn_slots = grad_chip[:tok_dev]
    for came in grad_came:
        grad_ffn_slots = low_sum(grad_ffn_slots, came)
    held = after(ffn_source, grad_chip)
    rows_first = Layout(major_to_minor=(0, 1))
    grad_w_gate = with_layout_constraint(left_transposed(held, grad_gate_low), rows_first)
    grad_w_up = with_layout_constraint(left_transposed(after(held, grad_came[0]), grad_up_low), rows_first)
    grad_down = left_transposed(after(hidden_low, grad_came[0]), grad_branch_rows)
    grad_down = grad_down.reshape(n_zh, n_y, units, width)

    grad_hidden_one, grad_gains, grad_query_gain, grad_attn_low, kv_part, grad_query_lin = on_chip(
        attend_back_kernel,
        (
            shaped(tok_dev, width, F32),
            shaped(8, width, F32),
            shaped(8, HD, F32),
            shaped(tok_dev, width, BF16),
            shaped(row_len, 2 * HD, F32),
            shaped(tok_dev, QW, BF16),
        ),
        after(grad_ffn_slots, grad_w_up, grad_down), hot_f, hidden_one, branch_attn, cotangent, gains, gains_h, full_w,
        hot_o, query_low, row_kv, probs, qk_lin, cosine, sine, outside=7, scratch=out_scratch,
    )
    out_chip = scatter_blocks(
        left_transposed(out_slots, grad_attn_low), 2, lambda v, j: move(v, dcore=j)
    )
    out_near = scatter_halves(out_chip)
    rows_y = width // n_y
    gate_came = [
        after(move(grad_w_gate[j * rows_y : (j + 1) * rows_y].astype(BF16), dy=j), grad_query_lin)
        for j in range(1, n_y)
    ]
    grad_kv = scatter_blocks(after(kv_part, *gate_came), n_ctx, swap_c)
    gate_y = grad_w_gate[:rows_y]
    for came in gate_came:
        gate_y = low_sum(gate_y, came)
    grad_qkv_low, chip_mine, chip_sent = on_chip(
        project_back_kernel,
        (
            shaped(tok_dev, n_qkv, BF16),
            shaped(half_w, n_wide, F32),
            shaped(half_w, n_wide, BF16),
        ),
        after(grad_kv, gate_y, out_chip), qk_lin, gains_h, cosine, sine, grad_query_lin, normed_slots,
        hot_w, hot_q, grad_gains, grad_ffn_post[None, :], grad_query_gain,
    )
    up_y = scatter_blocks(
        after(grad_w_up, gate_y), n_y, lambda v, j: after(move(after(v, grad_kv), dy=j), grad_qkv_low)
    )
    chip_w = low_sum(chip_mine, move(chip_sent, dcore=1))
    rows_n = chip_w.shape[0] // 4
    chip_low = after(chip_w, up_y).astype(BF16)
    chip_sent_x = jnp.concatenate([chip_low[rows_n : 2 * rows_n], chip_low[3 * rows_n :]], axis=0)
    chip_came = move(chip_sent_x, dx=1)
    chip_passed = low_sum(chip_w[2 * rows_n : 3 * rows_n], chip_came[rows_n:]).astype(BF16)
    down_y = pick(grad_down, y, 1)
    for j in range(1, n_y):
        sent = after(pick(grad_down, y ^ j, 1).astype(BF16), up_y)
        down_y = low_sum(down_y, after(move(sent, dy=j), chip_passed))
    near_w = low_sum(
        low_sum(chip_w[:rows_n], chip_came[:rows_n]), move(after(chip_passed, down_y), dzl=1)
    )
    mine_w = scatter_t(jnp.concatenate([near_w, out_near], axis=1))
    out_w_out = mine_w[:rows_o, n_wide:]
    sums = [
        scatter_blocks(gate_y, n_zh, lambda v, j: after(move(v, dzh=j), near_w)),
        scatter_blocks(up_y, n_zh, lambda v, j: after(move(v, dzh=j), near_w)),
    ]
    sums = jnp.stack([v.astype(BF16).reshape(4, 2, rows_w, cols) for v in sums], axis=1)
    owned = jnp.stack([near(pick(sums, zx ^ k), k) if k else pick(sums, zx) for k in range(4)])
    mine = pick(owned, core, 2)
    other = move(pick(owned, 1 - core, 2), dcore=1)
    out_gate, out_up = join_columns(mine, other, zx, core, n_t, n_y, units)
    out_down = pick(down_y, zh)
    for j in range(1, n_zh):
        out_down = low_sum(out_down, move(pick(down_y, zh ^ j).astype(BF16), dzh=j))
    grad_normed = right_transposed(
        right_transposed(after(grad_qkv_low, chip_w), full_qkv).astype(BF16), hot_w
    )
    grad_in_part, _ = norm_back(layer_in, gains[0], grad_normed)
    input_grad = (grad_hidden_one + grad_in_part).astype(BF16)
    out_gain_in = jnp.sum(w_rows.astype(F32) * mine_w[:, :n_qkv], axis=1) / gain_in.astype(F32)
    gain_out = mine_w[:, n_qkv:n_wide]
    return (
        layer_out,
        input_grad,
        mine_w[:, :QW],
        mine_w[:, QW : QW + HD],
        mine_w[:, QW + HD : n_qkv],
        out_w_out,
        out_gate,
        out_up,
        out_down,
        out_gain_in,
        gain_out[:, 0],
        gain_out[:, 1],
        gain_out[:, 2],
        gain_out[:rows_q, 3],
        gain_out[:rows_q, 4],
    )


def solution(mesh):
    split = P(("dp", "ctx"), None)
    split_1d = P(("dp", "ctx"))
    in_specs = (split, P("dp", None)) + (split,) * 7 + (split_1d,) * 6 + (split,)
    out_specs = (split,) * 9 + (split_1d,) * 6
    return jax.shard_map(body, mesh=mesh, in_specs=in_specs, out_specs=out_specs, check_vma=False)
```

```python
import jax
import jax.numpy as jnp
from jax import lax
from jax.experimental import pallas as pl
from jax.experimental.layout import Layout, with_layout_constraint
from jax.experimental.pallas import tpu as pltpu
from jax.sharding import PartitionSpec as P

HEADS = 4
HD = 256
QW = HEADS * HD


NORM_EPS = 1e-06
ROPE_BASE = 1000000.0
MASKED_SCORE = -1e30
F32 = jnp.float32
BF16 = jnp.bfloat16


def rms_norm(values_in, gain):
    return (
        values_in
        * lax.rsqrt(jnp.mean(values_in * values_in, axis=-1, keepdims=True) + NORM_EPS)
        * gain
    )


def places_of(owner, inner, tok_dev, n_ctx):
    half_len = tok_dev // 2
    block_id = jnp.where(inner < half_len, owner, 2 * n_ctx - 1 - owner)
    return block_id * half_len + inner % half_len


def segment_info(places, seq_lengths):
    ends = jnp.cumsum(seq_lengths)
    passed = places[:, None] >= ends[None, :]
    segment = jnp.sum(passed.astype(jnp.int32), axis=-1)
    start = jnp.sum(jnp.where(passed, seq_lengths[None, :], 0), axis=-1)
    return (segment, places - start)


def rope_tables(relative):
    head_half = HD // 2
    freqs = ROPE_BASE ** (-(jnp.arange(head_half, dtype=F32) * 2.0 / HD))
    angles = relative.astype(F32)[:, None] * freqs[None, :]
    cosine = jnp.concatenate([jnp.cos(angles), jnp.cos(angles)], axis=-1)
    sine = jnp.concatenate([jnp.sin(angles), jnp.sin(angles)], axis=-1)
    return (cosine, sine)


def rotate(values_in, cosine, sine):
    head_half = values_in.shape[-1] // 2
    turned = jnp.concatenate([-values_in[..., head_half:], values_in[..., :head_half]], axis=-1)
    return values_in * cosine + turned * sine


def ffn_piece(gate, upward):
    return jax.nn.gelu(gate, approximate=True) * upward


def matmul_fast(left, right):
    return jnp.dot(left, right, preferred_element_type=F32)


def left_transposed(left, right):
    return jnp.einsum("ta,tb->ab", left, right, preferred_element_type=F32)


def right_transposed(left, right):
    return jnp.einsum("ta,ba->tb", left, right, preferred_element_type=F32)


def dot(left, right, left_dim, right_dim):
    return lax.dot_general(
        left, right, (((left_dim,), (right_dim,)), ((), ())), preferred_element_type=F32
    )


def inverse_rms(values_in):
    return lax.rsqrt(jnp.mean(values_in * values_in, axis=-1, keepdims=True) + NORM_EPS)


def norm_back(values_in, gain, grad):
    inverse = inverse_rms(values_in)
    unit = values_in * inverse
    scaled = grad * gain
    grad_in = inverse * (scaled - unit * jnp.mean(scaled * unit, axis=-1, keepdims=True))
    return grad_in, jnp.sum(grad * unit, axis=0, keepdims=True)


def rotate_back(grad, cosine, sine):
    half = grad.shape[-1] // 2
    turned = grad * sine
    return grad * cosine + jnp.concatenate([turned[:, half:], -turned[:, :half]], axis=-1)


def head(h):
    return slice(h * HD, (h + 1) * HD)


def on_chip(kernel, out_shape, *operands, outside=None, scratch=()):
    vmem = pl.BlockSpec(memory_space=pltpu.VMEM)
    kept = pl.BlockSpec(memory_space=pl.ANY)
    return pl.pallas_call(
        kernel,
        out_shape=out_shape,
        in_specs=[kept if i == outside else vmem for i in range(len(operands))],
        scratch_shapes=scratch,
        out_specs=jax.tree.map(lambda _: vmem, out_shape),
        name=kernel.__name__,
    )(*operands)


def shaped(rows, columns, dtype):
    return jax.ShapeDtypeStruct((rows, columns), dtype)


def project_kernel(
    tok, w_outside, hot, hot_q, cosine, sine, slots, query, kv, lin, gains, gains_h, w, w_gains, sems
):
    n_qkv = QW + 2 * HD
    fetch_gains = pltpu.make_async_copy(
        w_outside.at[:, n_qkv : n_qkv + 128], w_gains, sems.at[0]
    )
    fetch = pltpu.make_async_copy(w_outside.at[:, :n_qkv], w, sems.at[1])
    fetch_gains.start()
    fetch.start()
    fetch_gains.wait()
    gain_rows = w_gains[...]
    all_gains = dot(gain_rows, hot[...], 0, 1)
    all_gains_h = dot(gain_rows, hot_q[...], 0, 1)
    gains[...] = all_gains[:8]
    gains_h[...] = all_gains_h[:8]
    layer_in = tok[...].astype(F32)
    normed = (layer_in * inverse_rms(layer_in) * all_gains[0:1]).astype(BF16)
    normed_slots = dot(normed, hot[...], 1, 0).astype(BF16)
    slots[...] = normed_slots
    fetch.wait()
    qkv = dot(normed_slots, w[...], 1, 0)
    lin[...] = qkv[:, : QW + HD]
    rows = tok.shape[0]

    def turned(values_in, gain):
        return rotate(values_in * inverse_rms(values_in) * gain, cosine[...], sine[...])

    for h in range(HEADS):
        query[h * rows : (h + 1) * rows, :] = turned(qkv[:, head(h)], all_gains_h[4:5]).astype(BF16)
    kv[:, :HD] = turned(qkv[:, head(HEADS)], all_gains_h[5:6]).astype(BF16)
    kv[:, HD:] = qkv[:, head(HEADS + 1)].astype(BF16)


def attend_kernel(
    query, kv, allowed, hot_o, w_outside, tok, gains, hot_f,
    probs, out_slots, branch, hidden_one, ffn_slots, w, sem,
):
    fetch = pltpu.make_async_copy(w_outside.at[:, QW + 2 * HD + 128 :], w, sem)
    fetch.start()
    rows = tok.shape[0]
    mask = allowed[...] > 0
    total = jnp.zeros(out_slots.shape, F32)
    for h in range(HEADS):
        part = slice(h * rows, (h + 1) * rows)
        raw = dot(query[part, :], kv[:, :HD], 1, 1) * HD ** (-0.5)
        scores = jnp.where(mask, raw, MASKED_SCORE)
        expo = jnp.exp(scores - jnp.max(scores, axis=-1, keepdims=True))
        prob = expo / jnp.sum(expo, axis=-1, keepdims=True)
        probs[part, :] = prob
        attended = dot(prob.astype(BF16), kv[:, HD:], 1, 0).astype(BF16)
        total += dot(attended, hot_o[head(h), :], 1, 0)
    total = total.astype(BF16)
    out_slots[...] = total
    fetch.wait()
    y = dot(total, w[...], 1, 0)
    branch[...] = y
    one = tok[...].astype(F32) + y * inverse_rms(y) * gains[1:2, :]
    hidden_one[...] = one
    ffn_in = (one * inverse_rms(one) * gains[2:3, :]).astype(BF16)
    ffn_slots[...] = dot(ffn_in, hot_f[...], 1, 0).astype(BF16)


def attend_back_kernel(
    grad_slots, hot_f, hidden_one, branch, cotangent, gains, gains_h, w_outside, hot_o,
    query, kv, probs, lin, cosine, sine,
    grad_one, grad_gains, grad_query_gain, grad_branch, kv_part, grad_lin, w, sem,
):
    fetch = pltpu.make_async_copy(w_outside.at[:, QW + 2 * HD + 128 :], w, sem)
    fetch.start()
    rows = cotangent.shape[0]
    grad_in = dot(grad_slots[...].astype(BF16), hot_f[...], 1, 1)
    part, gain_pre = norm_back(hidden_one[...], gains[2:3, :], grad_in)
    one = cotangent[...].astype(F32) + part
    grad_one[...] = one
    grad_y, gain_post = norm_back(branch[...], gains[1:2, :], one)
    grad_gains[...] = jnp.concatenate(
        [gain_post, gain_pre, jnp.zeros((6, gain_pre.shape[1]), F32)], axis=0
    )
    grad_y = grad_y.astype(BF16)
    grad_branch[...] = grad_y
    fetch.wait()
    grad_slots_o = dot(grad_y, w[...], 1, 1).astype(BF16)
    keys, values = kv[:, :HD], kv[:, HD:]
    grad_keys = jnp.zeros(keys.shape, F32)
    grad_values = jnp.zeros(values.shape, F32)
    gain_sum = jnp.zeros((1, HD), F32)
    for h in range(HEADS):
        span = slice(h * rows, (h + 1) * rows)
        grad_o = dot(grad_slots_o, hot_o[head(h), :], 1, 1).astype(BF16)
        prob = probs[span, :]
        grad_prob = dot(grad_o, values, 1, 1)
        delta = jnp.sum(grad_prob * prob, axis=-1, keepdims=True)
        grad_score = (prob * (grad_prob - delta)).astype(BF16)
        grad_keys += dot(grad_score, query[span, :], 0, 0)
        grad_values += dot(prob.astype(BF16), grad_o, 0, 0)
        grad_query = rotate_back(
            dot(grad_score, keys, 1, 0) * HD ** (-0.5), cosine[...], sine[...]
        )
        grad_head, gain = norm_back(lin[:, head(h)], gains_h[4:5, :], grad_query)
        gain_sum += gain
        grad_lin[:, head(h)] = grad_head.astype(BF16)
    kv_part[:, :HD] = grad_keys * HD ** (-0.5)
    kv_part[:, HD:] = grad_values
    grad_query_gain[...] = jnp.concatenate([gain_sum, jnp.zeros((7, HD), F32)], axis=0)


def project_back_kernel(
    grad_kv, lin, gains_h, cosine, sine, grad_query_lin, slots, hot, hot_q, grad_gains,
    grad_ffn_post, grad_query_gain, grad_lin, mine, sent,
):
    half = mine.shape[0]
    n_qkv = QW + 2 * HD
    grad_key, gain_key = norm_back(
        lin[:, QW:], gains_h[5:6, :], rotate_back(grad_kv[:, :HD], cosine[...], sine[...])
    )
    grad_lin[:, :QW] = grad_query_lin[...]
    grad_lin[:, head(HEADS)] = grad_key.astype(BF16)
    grad_lin[:, head(HEADS + 1)] = grad_kv[:, HD:].astype(BF16)
    grad_w = dot(slots[...], grad_lin[...], 0, 0)
    mine[:, :n_qkv] = grad_w[:half]
    sent[:, :n_qkv] = grad_w[half:].astype(BF16)
    wide = jnp.concatenate(
        [grad_gains[0:2, :], grad_ffn_post[...], jnp.zeros((125, hot.shape[0]), F32)], axis=0
    )
    narrow = jnp.concatenate(
        [jnp.zeros((3, HD), F32), grad_query_gain[0:1, :], gain_key, jnp.zeros((123, HD), F32)], axis=0
    )
    columns = dot(hot[...], wide.astype(BF16), 0, 1) + dot(hot_q[...], narrow.astype(BF16), 0, 1)
    mine[:, n_qkv:] = columns[:half]
    sent[:, n_qkv:] = columns[half:].astype(BF16)


def device_columns(k, c, t, n_y, units):
    start = (((t // n_y) * 4 + (k // 2) * 2 + c) * 2 * n_y + (t % n_y) * 2 + k % 2) * units
    return slice(start, start + units)


def split_columns(w_gate, w_up, core, n_t, n_y, units):
    rows = w_gate.shape[0]

    def kernel(core_ref, gate_ref, up_ref, out_ref):
        own = core_ref[0]
        for i, ref in enumerate((gate_ref, up_ref)):
            for c in range(2):
                for k in range(4):
                    for t in range(n_t):
                        out_ref[own ^ c, k, i, :, t * units : (t + 1) * units] = ref[
                            :, device_columns(k, c, t, n_y, units)
                        ]

    vmem = pl.BlockSpec(memory_space=pltpu.VMEM)
    return pl.pallas_call(
        kernel,
        out_shape=jax.ShapeDtypeStruct((2, 4, 2, rows, n_t * units), BF16),
        in_specs=[pl.BlockSpec(memory_space=pltpu.SMEM), vmem, vmem],
        out_specs=vmem,
        name="split_columns",
    )(jnp.reshape(core, (1,)), w_gate, w_up)


def join_columns(mine, other, zx, core, n_t, n_y, units):
    rows = mine.shape[2]

    def kernel(place_ref, mine_ref, other_ref, *outs):
        for i, out_ref in enumerate(outs):
            for k in range(4):
                own_core = mine_ref[place_ref[0] ^ k, i].astype(F32)
                other_core = other_ref[place_ref[0] ^ k, i].astype(F32)
                for c in range(2):
                    found = jnp.where(place_ref[1] == c, own_core, other_core)
                    for t in range(n_t):
                        out_ref[:, device_columns(k, c, t, n_y, units)] = found[
                            :, t * units : (t + 1) * units
                        ]

    vmem = pl.BlockSpec(memory_space=pltpu.VMEM)
    out = jax.ShapeDtypeStruct((rows, 8 * n_t * units), F32)
    return pl.pallas_call(
        kernel,
        out_shape=(out, out),
        in_specs=[pl.BlockSpec(memory_space=pltpu.SMEM), vmem, vmem],
        out_specs=(vmem, vmem),
        name="join_columns",
    )(jnp.stack([zx, core]), mine, other)


def body(
    tokens,
    lengths,
    w_query,
    w_key,
    w_value,
    w_out,
    w_gate,
    w_up,
    w_down,
    gain_in,
    gain_attn_post,
    gain_ffn_pre,
    gain_ffn_post,
    gain_query,
    gain_key,
    cotangent,
):
    n_ctx = lax.axis_size("ctx")
    n_dp = lax.axis_size("dp")
    n_y = n_ctx // 2
    n_zh = n_dp // 4
    n_t = n_y * n_zh
    n_dev = n_dp * n_ctx
    tok_dev, width = tokens.shape
    dp = lax.axis_index("dp")
    ctx = lax.axis_index("ctx")
    zh, zl, core = dp // 4, (dp // 2) % 2, dp % 2
    y, x = ctx // 2, ctx % 2
    zx = zl * 2 + x

    def move(values_in, dzh=0, dzl=0, dcore=0, dy=0, dx=0):
        pairs = [
            (d * n_ctx + c, (d ^ (4 * dzh + 2 * dzl + dcore)) * n_ctx + (c ^ (2 * dy + dx)))
            for d in range(n_dp)
            for c in range(n_ctx)
        ]
        return lax.ppermute(values_in, ("dp", "ctx"), pairs)

    def near(values_in, k):
        return move(values_in, dzl=k // 2, dx=k % 2)

    def pick(values_in, index, axis=0):
        return lax.dynamic_index_in_dim(values_in, index, axis, keepdims=False)

    def put(buffer, values_in, index, axis=0):
        return lax.dynamic_update_index_in_dim(buffer, values_in, index, axis)

    def after(values_in, *others):
        return lax.optimization_barrier((values_in,) + others)[0]

    def gather_zh(rows):
        return after(
            jnp.concatenate([rows] + [move(rows, dzh=j) for j in range(1, n_zh)], axis=0)
        )

    def gather_y(rows):
        return after(jnp.concatenate([rows] + [move(rows, dy=j) for j in range(1, n_y)], axis=0))

    def gather_near(rows):
        return [rows] + [near(rows, k) for k in range(1, 4)]

    def join_cores(own):
        return jnp.concatenate(own + [move(p, dcore=1) for p in own], axis=0)

    def low_sum(total, got):
        return total + got.astype(F32)

    def scatter_blocks(values_in, n, send):
        rows = values_in.shape[0] // n
        total = values_in[:rows]
        for j in range(1, n):
            total = low_sum(total, send(values_in[j * rows : (j + 1) * rows].astype(BF16), j))
        return total

    def scatter_halves(values_in):
        rows = values_in.shape[0] // 4
        low = values_in.astype(BF16)
        sent = jnp.concatenate([low[rows : 2 * rows], low[3 * rows :]], axis=0)
        came = move(sent, dx=1)
        total = low_sum(values_in[:rows], came[:rows])
        passed = low_sum(values_in[2 * rows : 3 * rows], came[rows:])
        return low_sum(total, move(passed.astype(BF16), dzl=1))

    def scatter_y(values_in):
        return scatter_blocks(values_in, n_y, lambda v, j: move(v, dy=j))

    def scatter_zh(values_in):
        return scatter_blocks(values_in, n_zh, lambda v, j: move(v, dzh=j))

    def scatter_t(values_in):
        return scatter_zh(scatter_y(values_in))

    def gather_group(values_in):
        return join_cores(gather_near(values_in))

    rows_w = w_query.shape[0]
    rows_o = w_out.shape[0]
    rows_q = gain_query.shape[0]

    def column(gain):
        return jnp.pad(gain, (0, rows_w - gain.shape[0]))[:, None]

    gain_cols = jnp.concatenate(
        [
            column(g)
            for g in (gain_in, gain_attn_post, gain_ffn_pre, gain_ffn_post, gain_query, gain_key)
        ],
        axis=1,
    )
    w_rows = jnp.concatenate([w_query, w_key, w_value], axis=1)
    n_qkv = w_rows.shape[1]
    n_wide = n_qkv + 128
    payload = jnp.concatenate(
        [
            w_rows,
            jnp.pad(gain_cols, ((0, 0), (0, 128 - 6))),
            jnp.pad(w_out, ((0, rows_w - rows_o), (0, 0))),
        ],
        axis=1,
    )
    payload_zh = gather_zh(payload)
    payload_t = gather_y(payload_zh)

    slots = after(jnp.arange(n_dev, dtype=jnp.int32), payload_zh)

    def device_of(part_core, part_zx, part_t):
        part_zh, part_y = part_t % n_zh, part_t // n_zh
        slot_dp = (zh ^ part_zh) * 4 + (part_zx // 2) * 2 + part_core
        return slot_dp * n_ctx + (y ^ part_y) * 2 + part_zx % 2

    dev_all = device_of(core ^ (slots // (4 * n_t)), zx ^ ((slots // n_t) % 4), slots % n_t)
    dev_ffn = device_of(slots % 2, (slots // 2) % 4, slots // 8)

    def one_hot(total, rows, slot_dev, padded):
        inner = jnp.arange(padded, dtype=jnp.int32)[None, :]
        natural = jnp.where(inner < rows, slot_dev[:, None] * rows + inner, -1)
        picks = jnp.arange(total, dtype=jnp.int32)[:, None] == natural.reshape(1, -1)
        return picks.astype(BF16)

    hot_w = one_hot(width, rows_w, dev_all, rows_w)
    hot_q = one_hot(HD, rows_q, dev_all, rows_w)
    hot_o = one_hot(QW, rows_o, dev_all, rows_w)
    half_w = width // 2
    hot_o = after(hot_o)
    hot_f = one_hot(width, rows_w, dev_ffn, rows_w)
    hot_w, hot_f, hot_q = after((hot_w, hot_f, hot_q))

    down_own_y = [move(after(w_down, payload_t), dy=j) for j in range(1, n_y)]
    near_w = [payload_t, move(payload_t, dx=1), move(payload_t, dzl=1)]
    near_w.append(move(near_w[2], dx=1))
    down_zh = [move(after(w_down, payload_zh), dzh=j) for j in range(1, n_zh)]
    near_w[1] = after(near_w[1], *down_zh)
    near_w[3] = after(near_w[3], *down_own_y)
    full_w = join_cores(near_w)

    units = w_down.shape[0]
    cols = n_t * units

    blocks = split_columns(w_gate, w_up, core, n_t, n_y, units)
    kept = blocks[0]
    got = move(blocks[1], dcore=1)
    paired = jnp.where(
        core == 0, jnp.concatenate([kept, got], axis=2), jnp.concatenate([got, kept], axis=2)
    )
    group_rows = jnp.zeros((2, 4, 2 * rows_w, cols), BF16)
    for k in range(4):
        piece = pick(paired, zx ^ k)
        group_rows = put(group_rows, near(piece, k) if k else piece, zx ^ k, 1)
    group_rows = group_rows.reshape(2, 8 * rows_w, cols)

    down_zh = [after(p, full_w) for p in down_zh]

    def join_down(held_by, down_far):
        joined = jnp.zeros((n_zh, n_y, units, width), BF16)
        for j in range(n_y):
            line = [down_own_y[j - 1]] + down_far[j - 1] if j else [w_down] + down_zh
            for i in range(n_zh):
                part = after(line[i], held_by)[None, None]
                joined = lax.dynamic_update_slice(joined, part, (zh ^ i, y ^ j, 0, 0))
        return joined.reshape(cols, width)

    gate_zh = [move(group_rows[0], dzh=j) for j in range(1, n_zh)]
    up_zh = [move(group_rows[1], dzh=j) for j in range(1, n_zh)]
    full_w = after(full_w, *gate_zh)
    full_qkv = full_w[:, :n_qkv]
    gate_far = [[move(p, dy=j) for p in gate_zh] for j in range(1, n_y)]
    wide_y = [move(group_rows, dy=j) for j in range(1, n_y)]

    def join_groups(i, came_zh, far):
        parts = [group_rows[i]] + came_zh
        for own, forwarded in zip(wide_y, far):
            parts = parts + [own[i]] + forwarded
        return jnp.concatenate(parts, axis=0)

    seq_lengths = lengths[0]
    inner = jnp.arange(tok_dev, dtype=jnp.int32)
    local_places = places_of(jnp.full_like(inner, ctx), inner, tok_dev, n_ctx)
    row_owner = ctx ^ jnp.arange(n_ctx, dtype=jnp.int32)
    row_places = places_of(row_owner[:, None], inner[None, :], tok_dev, n_ctx).reshape(-1)
    local_segment, local_relative = segment_info(local_places, seq_lengths)
    row_segment, row_relative = segment_info(row_places, seq_lengths)
    cosine, sine = rope_tables(local_relative)

    def swap_c(values_in, j):
        return move(values_in, dy=j // 2, dx=j % 2)

    layer_in = tokens.astype(F32)
    row_len = n_ctx * tok_dev
    normed_slots, query_low, own_kv, qk_lin, gains, gains_h = on_chip(
        project_kernel,
        (
            shaped(tok_dev, width, BF16),
            shaped(HEADS * tok_dev, HD, BF16),
            shaped(tok_dev, 2 * HD, BF16),
            shaped(tok_dev, QW + HD, F32),
            shaped(8, width, F32),
            shaped(8, HD, F32),
        ),
        tokens, after(full_w, *wide_y), hot_w, hot_q, cosine, sine,
        outside=1,
        scratch=[
            pltpu.VMEM((width, n_qkv), BF16),
            pltpu.VMEM((width, 128), BF16),
            pltpu.SemaphoreType.DMA((2,)),
        ],
    )
    out_scratch = [pltpu.VMEM((width, width), BF16), pltpu.SemaphoreType.DMA]
    row_kv = jnp.concatenate([own_kv] + [swap_c(own_kv, j) for j in range(1, n_ctx)], axis=0)
    up_zh = [after(p, row_kv) for p in up_zh]
    down_far = [[move(after(p, row_kv), dy=j) for p in down_zh] for j in range(1, n_y)]
    allowed = (local_segment[:, None] == row_segment[None, :]) & (
        row_places[None, :] <= local_places[:, None]
    )
    up_far = [[move(p, dy=j) for p in up_zh] for j in range(1, n_y)]
    probs, out_slots, branch_attn, hidden_one, ffn_slots = on_chip(
        attend_kernel,
        (
            shaped(HEADS * tok_dev, row_len, F32),
            shaped(tok_dev, width, BF16),
            shaped(tok_dev, width, F32),
            shaped(tok_dev, width, F32),
            shaped(tok_dev, width, BF16),
        ),
        after(query_low, *up_zh), after(row_kv, *sum(gate_far, [])), allowed.astype(F32), hot_o, full_w,
        tokens, gains, hot_f, outside=4, scratch=out_scratch,
    )

    half = 4 * tok_dev

    def scatter_group(left, right):
        far = right(left[half:]).astype(BF16)
        total = low_sum(right(left[:half]), move(far, dcore=1))
        return scatter_blocks(total, 4, near)

    ffn_source = gather_group(ffn_slots)
    full_gate = join_groups(0, gate_zh, gate_far)
    full_up = join_groups(1, up_zh, up_far)
    gate = matmul_fast(ffn_source, full_gate)
    upward = matmul_fast(ffn_source, full_up)
    full_down = after(join_down(upward, down_far))
    hidden, pull_ffn = jax.vjp(ffn_piece, gate, upward)
    hidden_low = hidden.astype(BF16)
    branch_ffn = scatter_group(hidden_low, lambda v: matmul_fast(v, full_down))
    post_ffn, pull_ffn_post = jax.vjp(rms_norm, branch_ffn, gains[3])
    layer_out = (hidden_one + post_ffn).astype(BF16)

    grad_out = cotangent.astype(F32)
    grad_branch_ffn, grad_ffn_post = pull_ffn_post(grad_out)
    grad_branch_rows = gather_group(grad_branch_ffn.astype(BF16))
    grad_hidden = right_transposed(grad_branch_rows, full_down)
    grad_gate, grad_upward = pull_ffn(grad_hidden)
    grad_gate_low = grad_gate.astype(BF16)
    grad_up_low = grad_upward.astype(BF16)

    def grad_terms(part):
        return right_transposed(grad_gate_low[part], full_gate) + right_transposed(
            grad_up_low[part], full_up
        )

    grad_far = move(grad_terms(slice(half, None)).astype(BF16), dcore=1)
    grad_chip = low_sum(grad_terms(slice(None, half)), grad_far)
    grad_came = [
        near(grad_chip[j * tok_dev : (j + 1) * tok_dev].astype(BF16), j) for j in range(1, 4)
    ]
    grad_ffn_slots = grad_chip[:tok_dev]
    for came in grad_came:
        grad_ffn_slots = low_sum(grad_ffn_slots, came)
    held = after(ffn_source, grad_chip)
    rows_first = Layout(major_to_minor=(0, 1))
    grad_w_gate = with_layout_constraint(left_transposed(held, grad_gate_low), rows_first)
    grad_w_up = with_layout_constraint(left_transposed(after(held, grad_came[0]), grad_up_low), rows_first)
    grad_down = left_transposed(after(hidden_low, grad_came[0]), grad_branch_rows)
    grad_down = grad_down.reshape(n_zh, n_y, units, width)

    grad_hidden_one, grad_gains, grad_query_gain, grad_attn_low, kv_part, grad_query_lin = on_chip(
        attend_back_kernel,
        (
            shaped(tok_dev, width, F32),
            shaped(8, width, F32),
            shaped(8, HD, F32),
            shaped(tok_dev, width, BF16),
            shaped(row_len, 2 * HD, F32),
            shaped(tok_dev, QW, BF16),
        ),
        after(grad_ffn_slots, grad_w_up, grad_down), hot_f, hidden_one, branch_attn, cotangent, gains, gains_h, full_w,
        hot_o, query_low, row_kv, probs, qk_lin, cosine, sine, outside=7, scratch=out_scratch,
    )
    out_chip = scatter_blocks(
        left_transposed(out_slots, grad_attn_low), 2, lambda v, j: move(v, dcore=j)
    )
    out_near = scatter_halves(out_chip)
    rows_y = width // n_y
    gate_came = [
        after(move(grad_w_gate[j * rows_y : (j + 1) * rows_y].astype(BF16), dy=j), grad_query_lin)
        for j in range(1, n_y)
    ]
    grad_kv = scatter_blocks(after(kv_part, *gate_came), n_ctx, swap_c)
    gate_y = grad_w_gate[:rows_y]
    for came in gate_came:
        gate_y = low_sum(gate_y, came)
    grad_qkv_low, chip_mine, chip_sent = on_chip(
        project_back_kernel,
        (
            shaped(tok_dev, n_qkv, BF16),
            shaped(half_w, n_wide, F32),
            shaped(half_w, n_wide, BF16),
        ),
        after(grad_kv, gate_y, out_chip), qk_lin, gains_h, cosine, sine, grad_query_lin, normed_slots,
        hot_w, hot_q, grad_gains, grad_ffn_post[None, :], grad_query_gain,
    )
    up_y = scatter_blocks(
        after(grad_w_up, gate_y), n_y, lambda v, j: after(move(after(v, grad_kv), dy=j), grad_qkv_low)
    )
    chip_w = low_sum(chip_mine, move(chip_sent, dcore=1))
    rows_n = chip_w.shape[0] // 4
    chip_low = after(chip_w, up_y).astype(BF16)
    chip_sent_x = jnp.concatenate([chip_low[rows_n : 2 * rows_n], chip_low[3 * rows_n :]], axis=0)
    chip_came = move(chip_sent_x, dx=1)
    chip_passed = low_sum(chip_w[2 * rows_n : 3 * rows_n], chip_came[rows_n:]).astype(BF16)
    down_y = pick(grad_down, y, 1)
    for j in range(1, n_y):
        sent = after(pick(grad_down, y ^ j, 1).astype(BF16), up_y)
        down_y = low_sum(down_y, after(move(sent, dy=j), chip_passed))
    near_w = low_sum(
        low_sum(chip_w[:rows_n], chip_came[:rows_n]), move(after(chip_passed, down_y), dzl=1)
    )
    mine_w = scatter_t(jnp.concatenate([near_w, out_near], axis=1))
    out_w_out = mine_w[:rows_o, n_wide:]
    sums = [
        scatter_blocks(gate_y, n_zh, lambda v, j: after(move(v, dzh=j), near_w)),
        scatter_blocks(up_y, n_zh, lambda v, j: after(move(v, dzh=j), near_w)),
    ]
    sums = jnp.stack([v.astype(BF16).reshape(4, 2, rows_w, cols) for v in sums], axis=1)
    owned = jnp.stack([near(pick(sums, zx ^ k), k) if k else pick(sums, zx) for k in range(4)])
    mine = pick(owned, core, 2)
    other = move(pick(owned, 1 - core, 2), dcore=1)
    out_gate, out_up = join_columns(mine, other, zx, core, n_t, n_y, units)
    out_down = pick(down_y, zh)
    for j in range(1, n_zh):
        out_down = low_sum(out_down, move(pick(down_y, zh ^ j).astype(BF16), dzh=j))
    grad_normed = right_transposed(
        right_transposed(after(grad_qkv_low, chip_w), full_qkv).astype(BF16), hot_w
    )
    grad_in_part, _ = norm_back(layer_in, gains[0], grad_normed)
    input_grad = (grad_hidden_one + grad_in_part).astype(BF16)
    out_gain_in = jnp.sum(w_rows.astype(F32) * mine_w[:, :n_qkv], axis=1) / gain_in.astype(F32)
    gain_out = mine_w[:, n_qkv:n_wide]
    return (
        layer_out,
        input_grad,
        mine_w[:, :QW],
        mine_w[:, QW : QW + HD],
        mine_w[:, QW + HD : n_qkv],
        out_w_out,
        out_gate,
        out_up,
        out_down,
        out_gain_in,
        gain_out[:, 0],
        gain_out[:, 1],
        gain_out[:, 2],
        gain_out[:rows_q, 3],
        gain_out[:rows_q, 4],
    )


def solution(mesh):
    split = P(("dp", "ctx"), None)
    split_1d = P(("dp", "ctx"))
    in_specs = (split, P("dp", None)) + (split,) * 7 + (split_1d,) * 6 + (split,)
    out_specs = (split,) * 9 + (split_1d,) * 6
    return jax.shard_map(body, mesh=mesh, in_specs=in_specs, out_specs=out_specs, check_vma=False)
```
